512 devices in a mesh: tm: 64 (over y, x, core), src: 8 (over z).
Axes of the slice: x: 4, y: 8, z: 8, core: 2. Of those that a mesh axis runs over, the one named last changes fastest.
Arguments:
- src_partials: float32 [5, 786432], P(None, ('tm', 'src')), may hold values from -3 to 3
- att_geom: float32 [4, 786432], P(None, ('tm', 'src')), may hold values from -2.5 to 2.5
- spline_frac: float32 [786432], P(('tm', 'src')), may hold values from 0 to 1
- cal_partials: float32 [6, 786432], P(None, ('tm', 'src')), may hold values from -2 to 2
- residual: float32 [786432], P(('tm', 'src')), may hold values from -6 to 6
- weight: float32 [786432], P(('tm', 'src')), may hold values from 0.1 to 1
- source_ids: int32 [786432], P(('tm', 'src')), may hold values from 0 to 1023, as said below
- knot_ids: int32 [786432], P(('tm', 'src')), may hold values from 0 to 16380, as said below
- ccd_ids: int32 [786432], P(('tm', 'src')), may hold values from 0 to 255
Outputs:
- src_normal: float32 [5, 5, 524288], P(None, None, ('tm', 'src'))
- src_rhs: float32 [5, 524288], P(None, ('tm', 'src'))
- att_normal: float32 [4, 4, 4, 16384], P(None, None, None, 'tm')
- att_rhs: float32 [4, 16384], P(None, 'tm')
- cal_normal: float32 [6, 6, 16384], P(None, None, 'tm')
- cal_rhs: float32 [6, 16384], P(None, 'tm')
The draws below stay inside these ranges and needn't reach their ends.
Inputs may be any that keep to these rules, and one draw needn't show every extreme that they name: `source_ids`: within each block of 1536 observations (blocks in the order of the tm+src placement) the source numbers do not decrease. `knot_ids`: among the rows of one device, at most 48 fall in any one time segment (knot index // 256); within every source shard some time segment holds exactly 48 rows of every device of that shard.
All inputs are finite; a program needn't handle non-finite values.
Results may differ from the reference program's by a relative error of at most 0.00016.
Values sent between devices are 32-bit elements; how exact they have to be, the bound alone decides.
No kernel may reach another device: no remote copies, remote signals or barrier semaphores. Data moves between devices by JAX's collectives and lax.ppermute only.
A program may use at most 64 MiB of HBM per device.

```python
import math
import jax
import jax.numpy as jnp
from jax import lax

OBS_DEV = 1536
SRC_DEV = 1024
KNOT_DEV = 256
CAL_DEV = 256
SRCP = 5
ATTC = 4
CALP = 6
OBS = 786432
SOURCES = 524288
KNOTS = 16384
CAL_UNITS = 16384
CAP = 48
SRC_SHARDS = 8


def layout_pick(key):
    base_key = jax.random.fold_in(key, 7)
    group_base = jax.random.fold_in(key, 11)
    seg_count = KNOTS // KNOT_DEV

    def one_block(block_index):
        block_key = jax.random.fold_in(base_key, block_index)
        hot_segment = jax.random.randint(jax.random.fold_in(group_base, block_index % SRC_SHARDS), (), 0, seg_count).astype(jnp.int32)
        others = jax.random.permutation(jax.random.fold_in(block_key, 1), (seg_count - 1) * CAP)[:OBS_DEV - CAP] // CAP
        others = others.astype(jnp.int32)
        others = others + (others >= hot_segment).astype(jnp.int32)
        segment = jnp.concatenate([jnp.full((CAP,), 0, jnp.int32) + hot_segment, others])
        source_pick = jax.random.randint(jax.random.fold_in(block_key, 2), (OBS_DEV,), 0, SRC_DEV).astype(jnp.int32)
        offset_pick = jax.random.randint(jax.random.fold_in(block_key, 3), (OBS_DEV,), 0, KNOT_DEV).astype(jnp.int32)
        knot_pick = jnp.minimum(segment * KNOT_DEV + offset_pick, KNOTS - 4)
        by_source = jnp.argsort(source_pick, stable=True)
        return (source_pick[by_source], knot_pick[by_source])
    source_all, knot_all = jax.vmap(one_block)(jnp.arange(OBS // OBS_DEV, dtype=jnp.int32))
    return (source_all.reshape(-1).astype(jnp.int32), knot_all.reshape(-1).astype(jnp.int32))


def draw_source_ids(key, part):
    return layout_pick(key)[0]


def draw_knot_ids(key, part):
    return layout_pick(key)[1]


def touch_ends(entries, own_key, smallest, top_value):
    extent = entries.shape
    place = [jax.random.randint(jax.random.fold_in(own_key, axis), (), 0, extent[axis]) for axis in range(len(extent))]
    entries = entries.at[tuple(place)].set(smallest)
    longest = extent.index(max(extent))
    place[longest] = (place[longest] + 1) % extent[longest]
    return entries.at[tuple(place)].set(top_value)


def levels(own_key, dims, shards, smallest, top_value):
    loudness = 1.0
    for dim, shards_of in shards:
        draws = jax.random.uniform(jax.random.fold_in(jax.random.fold_in(own_key, 6), dim), (shards_of,), jnp.float32, smallest / len(shards), top_value / len(shards))
        loudness = loudness * jnp.repeat(jnp.exp(draws), dims[dim] // shards_of).reshape((-1,) + (1,) * (len(dims) - 1 - dim))
    return loudness


def bell_draw(stream_key, dims, scale, limit, cuts=(), kind=jnp.bfloat16):
    result = jax.random.normal(stream_key, dims, jnp.float32) * scale
    if len(cuts) > 0:
        result = levels(stream_key, dims, cuts, -0.22, 0.18) * result
    return jnp.clip(result, min=-limit, max=limit).astype(kind)


def setup_inputs(seed: int = 0) -> dict:
    arg_keys = jax.random.split(jax.random.key(seed), 10)
    src_partials = bell_draw(arg_keys[0], (SRCP, OBS), 0.5, 3.0, ((1, 512),), jnp.float32)
    att_geom = bell_draw(arg_keys[1], (ATTC, OBS), 0.25, 2.5, ((1, 512),), jnp.float32)
    spline_frac = jnp.clip(1.0 * jax.random.uniform(arg_keys[2], (OBS,), jnp.float32) ** levels(arg_keys[2], (OBS,), ((0, 512),), -0.2, 0.2), 0.0, 1.0)
    cal_partials = bell_draw(arg_keys[3], (CALP, OBS), 0.15, 2.0, ((1, 512),), jnp.float32)
    residual = bell_draw(arg_keys[4], (OBS,), 1.0, 6.0, ((0, 512),), jnp.float32)
    weight = jnp.clip(jnp.exp(math.log(1.0) - 2.3025851 * jax.random.uniform(arg_keys[5], (OBS,), jnp.float32) ** levels(arg_keys[5], (OBS,), ((0, 512),), -0.2, 0.2)), 0.1, 1.0)
    source_ids = draw_source_ids(jax.random.fold_in(arg_keys[9], 71), 0)
    knot_ids = draw_knot_ids(jax.random.fold_in(arg_keys[9], 71), 0)
    ccd_ids = touch_ends(jax.random.randint(arg_keys[8], (OBS,), 0, CAL_DEV), jax.random.fold_in(arg_keys[8], 1), 0, CAL_DEV - 1).astype(jnp.int32)
    return {"src_partials": src_partials, "att_geom": att_geom, "spline_frac": spline_frac, "cal_partials": cal_partials, "residual": residual, "weight": weight, "source_ids": source_ids, "knot_ids": knot_ids, "ccd_ids": ccd_ids}


def spline_basis(frac):
    remain = 1.0 - frac
    square = frac * frac
    cubic_term = square * frac
    return jnp.stack([remain * remain * remain / 6.0, (3.0 * cubic_term - 6.0 * square + 4.0) / 6.0, (-3.0 * cubic_term + 3.0 * square + 3.0 * frac + 1.0) / 6.0, cubic_term / 6.0])


def spline_rows(frac, geom):
    return spline_basis(frac)[:, None, :] * geom[None, :, :]


def reference(src_partials, att_geom, spline_frac, cal_partials, residual, weight, source_ids, knot_ids, ccd_ids):
    weighted = weight * residual
    src_count = src_partials.shape[0]
    position = lax.iota(jnp.int32, source_ids.shape[0])
    src_global = ((position // OBS_DEV) * SRC_DEV + source_ids).astype(jnp.int32)
    outer_terms = (src_partials[:, None, :] * src_partials[None, :, :] * weight).reshape(src_count * src_count, -1)
    src_normal = jax.ops.segment_sum(outer_terms.T, src_global, num_segments=SOURCES).T.reshape(src_count, src_count, SOURCES)
    src_rhs = jax.ops.segment_sum((src_partials * weighted).T, src_global, num_segments=SOURCES).T
    partials = spline_rows(spline_frac, att_geom)
    comp_count = att_geom.shape[0]
    band_parts = []
    for band_gap in range(4):
        band_sum = jnp.zeros((KNOTS, comp_count * comp_count), jnp.float32)
        for first_knot in range(4 - band_gap):
            pair_terms = (partials[first_knot][:, None, :] * partials[first_knot + band_gap][None, :, :] * weight).reshape(comp_count * comp_count, -1)
            band_sum = band_sum + jax.ops.segment_sum(pair_terms.T, knot_ids + first_knot, num_segments=KNOTS)
        band_parts.append(band_sum.T.reshape(comp_count, comp_count, KNOTS))
    att_normal = jnp.stack(band_parts, 0)
    rhs_sum = jnp.zeros((KNOTS, comp_count), jnp.float32)
    for first_knot in range(4):
        rhs_sum = rhs_sum + jax.ops.segment_sum((partials[first_knot] * weighted).T, knot_ids + first_knot, num_segments=KNOTS)
    att_rhs = rhs_sum.T
    cal_unit = ((knot_ids // KNOT_DEV) * CAL_DEV + ccd_ids).astype(jnp.int32)
    cal_count = cal_partials.shape[0]
    cal_terms = (cal_partials[:, None, :] * cal_partials[None, :, :] * weight).reshape(cal_count * cal_count, -1)
    cal_normal = jax.ops.segment_sum(cal_terms.T, cal_unit, num_segments=CAL_UNITS).T.reshape(cal_count, cal_count, CAL_UNITS)
    cal_rhs = jax.ops.segment_sum((cal_partials * weighted).T, cal_unit, num_segments=CAL_UNITS).T
    return (src_normal, src_rhs, att_normal, att_rhs, cal_normal, cal_rhs)
```

```python
import jax
import jax.numpy as jnp
from jax import lax
from jax.experimental import pallas as pl
from jax.experimental.pallas import tpu as pltpu
from jax.sharding import PartitionSpec as P

SRC_DEV = 1024
SEG = 256
LANES = 128
F32 = jnp.float32
BF16 = jnp.bfloat16

FIELDS = 14
HALO_FIELDS = 7
ATT_PAIRS = [(c, e) for c in range(4) for e in range(c, 4)]
CAL_PAIRS = [(p, q) for p in range(6) for q in range(p, 6)]
SRC_PAIRS = [(p, q) for p in range(5) for q in range(p, 5)]
GROUP_ROWS = [48, 40, 24, 16]
GROUP_START = [0, 48, 88, 112]
VMEM_LIMIT = 56 * 1024 * 1024


def nt_dot(left, right):
    return lax.dot_general(
        left, right, (((1,), (1,)), ((), ())), preferred_element_type=F32
    )


def split(x):
    high = x.astype(BF16)
    return high, (x - high.astype(F32)).astype(BF16)


def onehot(rows, first, ids):
    place = lax.broadcasted_iota(jnp.int32, (rows, ids.shape[1]), 0) + first
    return jnp.where(place == ids, 1.0, 0.0).astype(BF16)


def pack_kernel(geom, frac, cal, resid, weight, knot, ccd, out, hot_s, val_s):
    obs = knot.shape[1]
    segs = out.shape[0]
    chunk = 256
    blocks = obs // chunk
    knots = knot[...]
    seg = knots // SEG
    member = onehot(segs, 0, seg)
    before = lax.broadcasted_iota(jnp.int32, (chunk, chunk), 0) < lax.broadcasted_iota(
        jnp.int32, (chunk, chunk), 1
    )
    before = jnp.where(before, 1.0, 0.0).astype(BF16)
    counter = jnp.concatenate([before, jnp.ones((chunk, LANES), BF16)], 1)
    carry = jnp.zeros((segs, LANES), F32)
    ranks = []
    for b in range(blocks):
        here = member[:, b * chunk : (b + 1) * chunk]
        counts = jnp.dot(here, counter, preferred_element_type=F32)
        for half in range(chunk // LANES):
            cols = slice(half * LANES, (half + 1) * LANES)
            ranks.append(
                jnp.sum(here[:, cols].astype(F32) * (counts[:, cols] + carry), 0, keepdims=True)
            )
        carry = carry + counts[:, chunk:]
    rank = jnp.concatenate(ranks, 1).astype(jnp.int32)
    high = rank // 8
    low = rank - 8 * high
    third = high // 3
    high3 = high - 3 * third

    scale = jnp.sqrt(weight[...])
    geoms = geom[...] * scale
    cals = cal[...] * scale
    fields = [geoms[c : c + 1] for c in range(4)]
    fields += [frac[...], resid[...] * scale, (knots - SEG * seg).astype(F32)]
    fields += [cals[p : p + 1] for p in range(6)]
    fields += [ccd[...].astype(F32)]
    fields = jnp.concatenate(fields, 0)
    rounded = fields.astype(BF16).astype(F32)
    parts = (rounded, fields - rounded)
    low_is = lax.broadcasted_iota(jnp.int32, (8, obs), 0) == low
    low_is3 = [low_is & (high3 == h) for h in range(3)]
    zero = jnp.zeros((8, obs), F32)

    def spread(row, mask):
        return jnp.where(mask, row, 0.0)

    for i, part in enumerate(parts):
        rows = [part[f : f + 1] for f in range(FIELDS)]
        main = [spread(r, low_is) for r in rows] + [zero, zero]
        extra = [spread(rows[f], low_is3[h]) for f in range(2, HALO_FIELDS) for h in range(3)]
        extra = extra + [zero]
        for j in range(0, 16, 2):
            at = i * LANES + 8 * j
            val_s[0, at : at + 16, :] = jnp.concatenate(main[j : j + 2], 0).astype(BF16)
            val_s[1, at : at + 16, :] = jnp.concatenate(extra[j : j + 2], 0).astype(BF16)
    code = seg * 8 + high
    for j in range(0, 8 * segs, 64):
        hot_s[j : j + 64, :] = onehot(64, j, code)
    main = nt_dot(hot_s[...], val_s[0])
    main = main[:, :LANES] + main[:, LANES:]
    extra = nt_dot(onehot(2 * segs, 0, jnp.where(seg == segs - 1, -1, seg + 1 + segs * third)), val_s[1])
    extra = extra[:, :LANES] + extra[:, LANES:]
    lane = lax.broadcasted_iota(jnp.int32, (8 * segs, LANES), 1)
    shifted = jnp.concatenate([jnp.zeros((8, LANES), F32), main[:-8]], 0)
    shifted = pltpu.roll(shifted, 8 * FIELDS, 1)
    tiles = jnp.where(lane < 8 * FIELDS, main, shifted)
    out[...] = tiles.reshape(segs, 8, LANES)
    out[:, 6, :] = extra[:segs]
    out[:, 7, :] = extra[segs:]


def source_kernel(partials, resid, weight, ids, normal, rhs, left_s):
    obs = ids.shape[1]
    count = partials.shape[0]
    part = partials[...]
    rows = [part[p : p + 1] for p in range(count)]
    scaled = part * weight[...]
    scaled_rows = [scaled[p : p + 1] for p in range(count)]
    terms = [scaled_rows[p] * rows[q] for p, q in SRC_PAIRS]
    terms += [scaled_rows[p] * resid[...] for p in range(count)]
    terms += [jnp.zeros((32 - len(terms), obs), F32)]
    high, low = split(jnp.concatenate(terms, 0))
    left_s[0:32, :] = high
    left_s[32:64, :] = low
    left = left_s[...]
    step = 256
    for j in range(0, SRC_DEV, step):
        sums = nt_dot(left, onehot(step, j, ids[...]))
        sums = sums[:32] + sums[32:]
        for t, (p, q) in enumerate(SRC_PAIRS):
            normal[p, q : q + 1, j : j + step] = sums[t : t + 1]
            if p != q:
                normal[q, p : p + 1, j : j + step] = sums[t : t + 1]
        rhs[:, j : j + step] = sums[len(SRC_PAIRS) : len(SRC_PAIRS) + count]


def att_terms(rows, keep):
    geoms = [jnp.where(keep, rows[c], 0.0) for c in range(4)]
    frac, resid = rows[4], rows[5]
    remain = 1.0 - frac
    square = frac * frac
    cubic = square * frac
    basis = [
        remain * remain * remain * (1.0 / 6.0),
        (3.0 * cubic - 6.0 * square + 4.0) * (1.0 / 6.0),
        (-3.0 * cubic + 3.0 * square + 3.0 * frac + 1.0) * (1.0 / 6.0),
        cubic * (1.0 / 6.0),
    ]
    pairs = [geoms[c] * geoms[e] for c, e in ATT_PAIRS]
    weighted = [geoms[c] * resid for c in range(4)]
    terms = []
    for a in range(4):
        place = GROUP_START[a]
        for c in range(4):
            terms.append((place + c, basis[a] * weighted[c]))
        place = place + 4
        for d in range(4 - a):
            both = basis[a] * basis[a + d]
            for q in range(10):
                terms.append((place + q, both * pairs[q]))
            place = place + 10
        end = GROUP_START[a] + GROUP_ROWS[a]
        for t in range(place, end):
            terms.append((t, jnp.zeros_like(frac)))
    return terms


def time_kernel(got, out, att_f, halo_f, cal_f, att_l, halo_l, cal_l, knot_hot, halo_hot, ccd_hot):
    lane = lax.broadcasted_iota(jnp.int32, (8, LANES), 1)
    sub = lane % 8
    keep = sub < 6
    chunks = got.shape[0] * 8 // LANES
    halo_hot[0 : LANES - 16, :] = jnp.zeros((LANES - 16, halo_hot.shape[1]), BF16)
    for c in range(chunks):
        block = got[c * 16 : (c + 1) * 16].reshape(LANES, LANES)
        turned = block.T
        rows = [turned[8 * f : 8 * f + 8] for f in range(16)]
        for t, value in att_terms(rows, keep):
            att_f[c, pl.ds(t, 8, stride=LANES), :] = value
        cals = [jnp.where(keep, rows[7 + p], 0.0) for p in range(6)]
        terms = [cals[p] * cals[q] for p, q in CAL_PAIRS]
        terms += [cals[p] * rows[5] for p in range(6)]
        terms += [jnp.zeros_like(lane, F32)] * (32 - len(terms))
        for t, value in enumerate(terms):
            cal_f[c, pl.ds(t, 8, stride=32), :] = value
        halo = [rows[14], rows[15]]
        for h in range(2, HALO_FIELDS):
            value = jnp.zeros((8, LANES), F32)
            for r in range(6):
                moved = pltpu.roll(rows[(h - 2) * 3 + r % 3], LANES - (6 + r // 3 - r), 1)
                value = jnp.where(sub == r, moved, value)
            halo.append(value)
        for t, value in att_terms(halo, keep):
            halo_f[c, pl.ds(t, 8, stride=LANES), :] = value
        for l in range(8):
            cols = slice((c * 8 + l) * LANES, (c * 8 + l + 1) * LANES)
            att_l[0:LANES, cols], att_l[LANES:, cols] = split(att_f[c, l * LANES : (l + 1) * LANES, :])
            halo_l[0:LANES, cols], halo_l[LANES:, cols] = split(
                halo_f[c, l * LANES : (l + 1) * LANES, :]
            )
            cal_l[0:32, cols], cal_l[32:, cols] = split(cal_f[c, l * 32 : (l + 1) * 32, :])
            knot_hot[:, cols] = onehot(SEG, 0, rows[6][l : l + 1].astype(jnp.int32))
            ccd_hot[:, cols] = onehot(SEG, 0, rows[13][l : l + 1].astype(jnp.int32))
            halo_hot[LANES - 16 :, cols] = onehot(16, SEG - 16, halo[6][l : l + 1].astype(jnp.int32))
    main = nt_dot(att_l[...], knot_hot[...])
    edge = nt_dot(halo_l[...], halo_hot[...])
    sums = jnp.concatenate([edge[:LANES] + edge[LANES:], main[:LANES] + main[LANES:]], 1)
    total = sums[: GROUP_ROWS[0], LANES:]
    for a in range(1, 4):
        n = GROUP_ROWS[a]
        group = sums[GROUP_START[a] : GROUP_START[a] + n]
        group = pltpu.roll(group, a, 1)[:, LANES:]
        if n < GROUP_ROWS[0]:
            group = jnp.concatenate([group, jnp.zeros((GROUP_ROWS[0] - n, SEG), F32)], 0)
        total = total + group
    cal = nt_dot(cal_l[...], ccd_hot[...])
    cal = cal[:32] + cal[32:]
    for z in range(out.shape[0]):
        out[z, 0:48, :] = total
        out[z, 48:72, :] = cal[0:24]
        out[z, 44:47, :] = cal[24:27]


def final_kernel(parts, att_normal, att_rhs, cal_normal, cal_rhs, sum_s):
    total = parts[0]
    for z in range(1, parts.shape[0]):
        total = total + parts[z]
    sum_s[...] = total
    att_rhs[...] = sum_s[0:4, :]
    for d in range(4):
        for q, (c, e) in enumerate(ATT_PAIRS):
            row = sum_s[4 + 10 * d + q : 5 + 10 * d + q, :]
            att_normal[d, c, e : e + 1, :] = row
            if c != e:
                att_normal[d, e, c : c + 1, :] = row

    def cal_row(t):
        at = 48 + t if t < 24 else 20 + t
        return sum_s[at : at + 1, :]

    for t, (p, q) in enumerate(CAL_PAIRS):
        cal_normal[p, q : q + 1, :] = cal_row(t)
        if p != q:
            cal_normal[q, p : p + 1, :] = cal_row(t)
    for p in range(6):
        cal_rhs[p : p + 1, :] = cal_row(21 + p)


def call(kernel, out_shape, scratch, cost, *args):
    return pl.pallas_call(
        kernel,
        out_shape=out_shape,
        scratch_shapes=scratch,
        compiler_params=pltpu.CompilerParams(vmem_limit_bytes=VMEM_LIMIT),
        cost_estimate=pl.CostEstimate(flops=cost, bytes_accessed=200000, transcendentals=0),
    )(*args)


def shape(*dims):
    return jax.ShapeDtypeStruct(dims, F32)


def local(
    src_partials,
    att_geom,
    spline_frac,
    cal_partials,
    residual,
    weight,
    source_ids,
    knot_ids,
    ccd_ids,
):
    obs = residual.shape[0]
    tm_count = lax.axis_size("tm")
    z_count = lax.axis_size("src")
    frac, resid, wgt = (x.reshape(1, obs) for x in (spline_frac, residual, weight))
    ids, knots, ccds = (x.reshape(1, obs) for x in (source_ids, knot_ids, ccd_ids))
    send = call(
        pack_kernel,
        shape(tm_count, 8, LANES),
        [pltpu.VMEM((8 * tm_count, obs), BF16), pltpu.VMEM((2, 2 * LANES, obs), BF16)],
        1000000000,
        att_geom,
        frac,
        cal_partials,
        resid,
        wgt,
        knots,
        ccds,
    )
    got = lax.all_to_all(send, "tm", split_axis=0, concat_axis=0, tiled=True)
    src_normal, src_rhs = call(
        source_kernel,
        (shape(5, 5, SRC_DEV), shape(5, SRC_DEV)),
        [pltpu.VMEM((64, obs), BF16)],
        4000000000,
        src_partials,
        resid,
        wgt,
        ids,
    )
    depth = tm_count * 64
    chunks = tm_count * 8 // LANES
    sums = call(
        time_kernel,
        shape(z_count, 72, SEG),
        [
            pltpu.VMEM((chunks, 8 * LANES, LANES), F32),
            pltpu.VMEM((chunks, 8 * LANES, LANES), F32),
            pltpu.VMEM((chunks, 8 * 32, LANES), F32),
            pltpu.VMEM((2 * LANES, depth), BF16),
            pltpu.VMEM((2 * LANES, depth), BF16),
            pltpu.VMEM((64, depth), BF16),
            pltpu.VMEM((SEG, depth), BF16),
            pltpu.VMEM((LANES, depth), BF16),
            pltpu.VMEM((SEG, depth), BF16),
        ],
        1000000000,
        got,
    )
    parts = lax.all_to_all(sums, "src", split_axis=0, concat_axis=0, tiled=True)
    att_normal, att_rhs, cal_normal, cal_rhs = call(
        final_kernel,
        (shape(4, 4, 4, SEG), shape(4, SEG), shape(6, 6, SEG), shape(6, SEG)),
        [pltpu.VMEM((72, SEG), F32)],
        1000000,
        parts,
    )
    return (src_normal, src_rhs, att_normal, att_rhs, cal_normal, cal_rhs)


def solution(mesh):
    both = ("tm", "src")
    in_specs = (
        P(None, both),
        P(None, both),
        P(both),
        P(None, both),
        P(both),
        P(both),
        P(both),
        P(both),
        P(both),
    )
    out_specs = (
        P(None, None, both),
        P(None, both),
        P(None, None, None, "tm"),
        P(None, "tm"),
        P(None, None, "tm"),
        P(None, "tm"),
    )
    return jax.shard_map(local, mesh=mesh, in_specs=in_specs, out_specs=out_specs, check_vma=False)
```

```python
import jax
import jax.numpy as jnp
from jax import lax
from jax.experimental import pallas as pl
from jax.experimental.pallas import tpu as pltpu
from jax.sharding import PartitionSpec as P

SRC_DEV = 1024
SEG = 256
LANES = 128
F32 = jnp.float32
BF16 = jnp.bfloat16

LOW = 6
FIELDS = 14
HALO_FIELDS = 7
HALO_LANE = LOW * FIELDS
ATT_PAIRS = [(c, e) for c in range(4) for e in range(c, 4)]
CAL_PAIRS = [(p, q) for p in range(6) for q in range(p, 6)]
SRC_PAIRS = [(p, q) for p in range(5) for q in range(p, 5)]
GROUP_ROWS = [48, 40, 24, 16]
GROUP_START = [0, 48, 88, 112]
TERMS = 128
EDGE = TERMS - GROUP_START[1]


def nt_dot(left, right):
    return lax.dot_general(
        left, right, (((1,), (1,)), ((), ())), preferred_element_type=F32
    )


def split(x):
    high = x.astype(BF16)
    return high, (x - high.astype(F32)).astype(BF16)


def onehot(rows, first, ids):
    place = lax.broadcasted_iota(jnp.int32, (rows, ids.shape[1]), 0) + first
    return jnp.where(place == ids, 1.0, 0.0).astype(BF16)


def pack_kernel(*refs):
    count = 7
    hot_s, val_s = refs[count + 1 : count + 3]
    out = refs[count]
    held = refs[count + 3 : -1]
    copies = [
        pltpu.make_async_copy(refs[i], held[i], refs[-1].at[i]) for i in range(count)
    ]
    for copy in copies:
        copy.start()
    for copy in copies:
        copy.wait()
    geom, frac, cal, resid, weight, knot, ccd = held
    obs = knot.shape[0]
    segs = out.shape[0]
    chunk = 256
    blocks = obs // chunk
    knots = knot[...].reshape(1, obs)
    seg = knots // SEG
    member = onehot(segs, 0, seg)
    before = lax.broadcasted_iota(jnp.int32, (chunk, chunk), 0) < lax.broadcasted_iota(
        jnp.int32, (chunk, chunk), 1
    )
    before = jnp.where(before, 1.0, 0.0).astype(BF16)
    counter = jnp.concatenate([before, jnp.ones((chunk, LANES), BF16)], 1)
    carry = jnp.zeros((segs, LANES), F32)
    ranks = []
    for b in range(blocks):
        here = member[:, b * chunk : (b + 1) * chunk]
        counts = jnp.dot(here, counter, preferred_element_type=F32)
        for half in range(chunk // LANES):
            cols = slice(half * LANES, (half + 1) * LANES)
            ranks.append(
                jnp.sum(here[:, cols].astype(F32) * (counts[:, cols] + carry), 0, keepdims=True)
            )
        carry = carry + counts[:, chunk:]
    rank = jnp.concatenate(ranks, 1).astype(jnp.int32)
    high = (rank * 43) >> 8
    low = rank - LOW * high

    wgt = weight[...].reshape(1, obs)
    scale = jnp.sqrt(wgt)
    geoms = geom[...] * scale
    cals = cal[...] * scale
    fields = [geoms[c : c + 1] for c in range(4)]
    fields += [frac[...].reshape(1, obs), resid[...].reshape(1, obs) * scale]
    fields += [(knots - SEG * seg).astype(F32)]
    fields += [cals[p : p + 1] for p in range(6)]
    fields += [ccd[...].reshape(1, obs).astype(F32)]
    fields = jnp.concatenate(fields, 0)
    rounded = fields.astype(BF16).astype(F32)
    parts = (rounded, fields - rounded)
    sub = lax.broadcasted_iota(jnp.int32, (8, obs), 0)
    masks = [(sub + 8 * j) % LOW == low for j in range(3)]
    for i, part in enumerate(parts):
        tiles = []
        for j in range(LANES // 8):
            first, last = 8 * j // LOW, (8 * j + 7) // LOW
            if first >= FIELDS:
                tiles.append(jnp.zeros((8, obs), F32))
                continue
            value = jnp.broadcast_to(part[first : first + 1], (8, obs))
            for f in range(first + 1, last + 1):
                row = part[f : f + 1] if f < FIELDS else 0.0
                value = jnp.where(sub < LOW * f - 8 * j, value, row)
            tiles.append(jnp.where(masks[j % 3], value, 0.0))
        for j in range(0, LANES // 8, 2):
            at = i * LANES + 8 * j
            val_s[at : at + 16, :] = jnp.concatenate(tiles[j : j + 2], 0).astype(BF16)
    code = seg * 8 + high
    for j in range(0, 8 * segs, 64):
        hot_s[j : j + 64, :] = onehot(64, j, code)
    main = nt_dot(hot_s[...], val_s[...])
    main = main[:, :LANES] + main[:, LANES:]
    lane = lax.broadcasted_iota(jnp.int32, (8 * segs, LANES), 1)
    shifted = jnp.concatenate([jnp.zeros((8, LANES), F32), main[:-8]], 0)
    shifted = pltpu.roll(shifted, HALO_LANE, 1)
    out[...] = jnp.where(lane < HALO_LANE, main, shifted).reshape(segs, 8, LANES)


def source_kernel(partials, resid, weight, ids, normal, rhs, left_s):
    obs = ids.shape[0]
    wgt, res, idv = (x[...].reshape(1, obs) for x in (weight, resid, ids))
    count = partials.shape[0]
    part = partials[...]
    rows = [part[p : p + 1] for p in range(count)]
    scaled = part * wgt
    scaled_rows = [scaled[p : p + 1] for p in range(count)]
    terms = [scaled_rows[p] * rows[q] for p, q in SRC_PAIRS]
    terms += [scaled_rows[p] * res for p in range(count)]
    terms += [jnp.zeros((32 - len(terms), obs), F32)]
    high, low = split(jnp.concatenate(terms, 0))
    left_s[0:32, :] = high
    left_s[32:64, :] = low
    left = left_s[...]
    step = 256
    for j in range(0, SRC_DEV, step):
        sums = nt_dot(left, onehot(step, j, idv))
        sums = sums[:32] + sums[32:]
        for t, (p, q) in enumerate(SRC_PAIRS):
            normal[p, q : q + 1, j : j + step] = sums[t : t + 1]
            if p != q:
                normal[q, p : p + 1, j : j + step] = sums[t : t + 1]
        rhs[:, j : j + step] = sums[len(SRC_PAIRS) : len(SRC_PAIRS) + count]


def att_terms(rows, first):
    geoms = rows[:4]
    frac, resid = rows[4], rows[5]
    remain = 1.0 - frac
    square = frac * frac
    cubic = square * frac
    basis = [
        remain * remain * remain * (1.0 / 6.0),
        (3.0 * cubic - 6.0 * square + 4.0) * (1.0 / 6.0),
        (-3.0 * cubic + 3.0 * square + 3.0 * frac + 1.0) * (1.0 / 6.0),
        cubic * (1.0 / 6.0),
    ]
    pairs = [geoms[c] * geoms[e] for c, e in ATT_PAIRS]
    weighted = [geoms[c] * resid for c in range(4)]
    terms = []
    for a in range(first, 4):
        place = GROUP_START[a]
        for c in range(4):
            terms.append((place + c, basis[a] * weighted[c]))
        place = place + 4
        for d in range(4 - a):
            both = basis[a] * basis[a + d]
            for q in range(10):
                terms.append((place + q, both * pairs[q]))
            place = place + 10
        for t in range(place, GROUP_START[a] + GROUP_ROWS[a]):
            terms.append((t, jnp.zeros_like(frac)))
    return terms


def time_kernel(got, out, turned_s, att_f, halo_f, cal_f, att_l, halo_l, cal_l, knot_hot, halo_hot, ccd_hot):
    chunks = got.shape[0] * 8 // LANES
    for c in range(chunks):
        turned_s[c] = got[c * 16 : (c + 1) * 16].reshape(LANES, LANES).T
        rows = [turned_s[c, LOW * f : LOW * f + LOW, :] for f in range(FIELDS + HALO_FIELDS)]
        for t, value in att_terms(rows, 0):
            att_f[c, pl.ds(t, LOW, stride=TERMS), :] = value
        cals = rows[7:13]
        terms = [cals[p] * cals[q] for p, q in CAL_PAIRS]
        terms += [cals[p] * rows[5] for p in range(6)]
        terms += [jnp.zeros((LOW, LANES), F32)] * (32 - len(terms))
        for t, value in enumerate(terms):
            cal_f[c, pl.ds(t, LOW, stride=32), :] = value
        for t, value in att_terms(rows[FIELDS:], 1):
            halo_f[c, pl.ds(t - GROUP_START[1], LOW, stride=EDGE), :] = value
        for l in range(LOW):
            at = (c * LOW + l) * LANES
            cols = slice(at, at + LANES)
            att_l[0:TERMS, cols], att_l[TERMS:, cols] = split(att_f[c, l * TERMS : (l + 1) * TERMS, :])
            halo_l[0:EDGE, cols], halo_l[EDGE:, cols] = split(halo_f[c, l * EDGE : (l + 1) * EDGE, :])
            cal_l[0:32, cols], cal_l[32:, cols] = split(cal_f[c, l * 32 : (l + 1) * 32, :])

            def label(f):
                return turned_s[c, LOW * f + l : LOW * f + l + 1, :].astype(jnp.int32)

            knot_hot[:, cols] = onehot(SEG, 0, label(6))
            ccd_hot[:, cols] = onehot(SEG, 0, label(13))
            halo_hot[:, cols] = onehot(16, SEG - 16, label(FIELDS + 6))
    main = nt_dot(att_l[...], knot_hot[...])
    main = main[:TERMS] + main[TERMS:]
    edge = nt_dot(halo_l[...], halo_hot[...])
    edge = edge[:EDGE] + edge[EDGE:]
    edge = jnp.concatenate([jnp.zeros((EDGE, LANES - 16), F32), edge], 1)
    total = main[: GROUP_ROWS[0]]
    for a in range(1, 4):
        n = GROUP_ROWS[a]
        at = GROUP_START[a]
        group = jnp.concatenate([edge[at - GROUP_START[1] :][:n], main[at : at + n]], 1)
        group = pltpu.roll(group, a, 1)[:, LANES:]
        if n < GROUP_ROWS[0]:
            group = jnp.concatenate([group, jnp.zeros((GROUP_ROWS[0] - n, SEG), F32)], 0)
        total = total + group
    cal = nt_dot(cal_l[...], ccd_hot[...])
    cal = cal[:32] + cal[32:]
    for z in range(out.shape[0]):
        out[z, 0:48, :] = total
        out[z, 48:72, :] = cal[0:24]
        out[z, 44:47, :] = cal[24:27]


def final_kernel(parts, att_normal, att_rhs, cal_normal, cal_rhs, sum_s):
    total = parts[0]
    for z in range(1, parts.shape[0]):
        total = total + parts[z]
    sum_s[...] = total
    att_rhs[...] = sum_s[0:4, :]
    for d in range(4):
        for q, (c, e) in enumerate(ATT_PAIRS):
            row = sum_s[4 + 10 * d + q : 5 + 10 * d + q, :]
            att_normal[d, c, e : e + 1, :] = row
            if c != e:
                att_normal[d, e, c : c + 1, :] = row

    def cal_row(t):
        at = 48 + t if t < 24 else 20 + t
        return sum_s[at : at + 1, :]

    for t, (p, q) in enumerate(CAL_PAIRS):
        cal_normal[p, q : q + 1, :] = cal_row(t)
        if p != q:
            cal_normal[q, p : p + 1, :] = cal_row(t)
    for p in range(6):
        cal_rhs[p : p + 1, :] = cal_row(21 + p)


def call(kernel, out_shape, scratch, vmem_mib, cost, *args, space=pltpu.VMEM):
    return pl.pallas_call(
        kernel,
        out_shape=out_shape,
        in_specs=[pl.BlockSpec(memory_space=space)] * len(args),
        scratch_shapes=scratch,
        compiler_params=pltpu.CompilerParams(vmem_limit_bytes=vmem_mib * 1024 * 1024),
        cost_estimate=pl.CostEstimate(flops=cost, bytes_accessed=200000, transcendentals=0),
    )(*args)


def shape(*dims):
    return jax.ShapeDtypeStruct(dims, F32)


def local(
    src_partials,
    att_geom,
    spline_frac,
    cal_partials,
    residual,
    weight,
    source_ids,
    knot_ids,
    ccd_ids,
):
    obs = residual.shape[0]
    tm_count = lax.axis_size("tm")
    z_count = lax.axis_size("src")
    rows = (att_geom, spline_frac, cal_partials, residual, weight, knot_ids, ccd_ids)
    send = call(
        pack_kernel,
        shape(tm_count, 8, LANES),
        [pltpu.VMEM((8 * tm_count, obs), BF16), pltpu.VMEM((2 * LANES, obs), BF16)]
        + [pltpu.VMEM(x.shape, x.dtype) for x in rows]
        + [pltpu.SemaphoreType.DMA((len(rows),))],
        12,
        1000000000,
        *rows,
        space=pltpu.HBM,
    )
    got = lax.all_to_all(send, "tm", split_axis=0, concat_axis=0, tiled=True)
    src_normal, src_rhs = call(
        source_kernel,
        (shape(5, 5, SRC_DEV), shape(5, SRC_DEV)),
        [pltpu.VMEM((64, obs), BF16)],
        12,
        4000000000,
        src_partials,
        residual,
        weight,
        source_ids,
    )
    chunks = tm_count * 8 // LANES
    depth = chunks * LOW * LANES
    sums = call(
        time_kernel,
        shape(z_count, 72, SEG),
        [
            pltpu.VMEM((chunks, LANES, LANES), F32),
            pltpu.VMEM((chunks, LOW * TERMS, LANES), F32),
            pltpu.VMEM((chunks, LOW * EDGE, LANES), F32),
            pltpu.VMEM((chunks, LOW * 32, LANES), F32),
            pltpu.VMEM((2 * TERMS, depth), BF16),
            pltpu.VMEM((2 * EDGE, depth), BF16),
            pltpu.VMEM((64, depth), BF16),
            pltpu.VMEM((SEG, depth), BF16),
            pltpu.VMEM((16, depth), BF16),
            pltpu.VMEM((SEG, depth), BF16),
        ],
        24,
        1000000000,
        got,
    )
    parts = lax.all_to_all(sums, "src", split_axis=0, concat_axis=0, tiled=True)
    att_normal, att_rhs, cal_normal, cal_rhs = call(
        final_kernel,
        (shape(4, 4, 4, SEG), shape(4, SEG), shape(6, 6, SEG), shape(6, SEG)),
        [pltpu.VMEM((72, SEG), F32)],
        8,
        1000000,
        parts,
    )
    return (src_normal, src_rhs, att_normal, att_rhs, cal_normal, cal_rhs)


def solution(mesh):
    both = ("tm", "src")
    in_specs = (
        P(None, both),
        P(None, both),
        P(both),
        P(None, both),
        P(both),
        P(both),
        P(both),
        P(both),
        P(both),
    )
    out_specs = (
        P(None, None, both),
        P(None, both),
        P(None, None, None, "tm"),
        P(None, "tm"),
        P(None, None, "tm"),
        P(None, "tm"),
    )
    return jax.shard_map(local, mesh=mesh, in_specs=in_specs, out_specs=out_specs, check_vma=False)
```

```python
import jax
import jax.numpy as jnp
from jax import lax
from jax.experimental import pallas as pl
from jax.experimental.pallas import tpu as pltpu
from jax.sharding import PartitionSpec as P

SRC_DEV = 1024
SEG = 256
LANES = 128
F32 = jnp.float32
BF16 = jnp.bfloat16

LOW = 6
FIELDS = 14
HALO_FIELDS = 7
HALO_LANE = LOW * FIELDS
ATT_PAIRS = [(c, e) for c in range(4) for e in range(c, 4)]
CAL_PAIRS = [(p, q) for p in range(6) for q in range(p, 6)]
SRC_PAIRS = [(p, q) for p in range(5) for q in range(p, 5)]
GROUP_ROWS = [48, 40, 24, 16]
GROUP_START = [0, 48, 88, 112]
TERMS = 128
PACK_MIB = 56
EDGE = TERMS - GROUP_START[1]


def nt_dot(left, right):
    return lax.dot_general(
        left, right, (((1,), (1,)), ((), ())), preferred_element_type=F32
    )


def split(x):
    high = x.astype(BF16)
    return high, (x - high.astype(F32)).astype(BF16)


def onehot(rows, first, ids):
    place = lax.broadcasted_iota(jnp.int32, (rows, ids.shape[1]), 0) + first
    return jnp.where(place == ids, 1.0, 0.0).astype(BF16)


def pack_kernel(*refs):
    count = 7
    hot_s, val_s = refs[count + 1 : count + 3]
    out = refs[count]
    held = refs[count + 3 : -1]
    copies = [
        pltpu.make_async_copy(refs[i], held[i], refs[-1].at[i]) for i in range(count)
    ]
    for i in (5, 0, 1, 2, 3, 4, 6):
        copies[i].start()
    geom, frac, cal, resid, weight, knot, ccd = held
    copies[5].wait()
    obs = knot.shape[0]
    segs = out.shape[0]
    chunk = 256
    blocks = obs // chunk
    knots = knot[...].reshape(1, obs)
    seg = knots // SEG
    member = onehot(segs, 0, seg)
    before = lax.broadcasted_iota(jnp.int32, (chunk, chunk), 0) < lax.broadcasted_iota(
        jnp.int32, (chunk, chunk), 1
    )
    before = jnp.where(before, 1.0, 0.0).astype(BF16)
    counter = jnp.concatenate([before, jnp.ones((chunk, LANES), BF16)], 1)
    carry = jnp.zeros((segs, LANES), F32)
    ranks = []
    for b in range(blocks):
        here = member[:, b * chunk : (b + 1) * chunk]
        counts = jnp.dot(here, counter, preferred_element_type=F32)
        for half in range(chunk // LANES):
            cols = slice(half * LANES, (half + 1) * LANES)
            ranks.append(
                jnp.sum(here[:, cols].astype(F32) * (counts[:, cols] + carry), 0, keepdims=True)
            )
        carry = carry + counts[:, chunk:]
    rank = jnp.concatenate(ranks, 1).astype(jnp.int32)
    high = (rank * 43) >> 8
    low = rank - LOW * high

    for i in (0, 1, 2, 3, 4, 6):
        copies[i].wait()
    scale = jnp.sqrt(weight[...].reshape(1, obs))
    geoms = geom[...] * scale
    cals = cal[...] * scale
    fields = [geoms[c : c + 1] for c in range(4)]
    fields += [frac[...].reshape(1, obs), resid[...].reshape(1, obs) * scale]
    fields += [(knots - SEG * seg).astype(F32)]
    fields += [cals[p : p + 1] for p in range(6)]
    fields += [ccd[...].reshape(1, obs).astype(F32)]
    fields = jnp.concatenate(fields, 0)
    rounded = fields.astype(BF16).astype(F32)
    parts = (rounded, fields - rounded)
    sub = lax.broadcasted_iota(jnp.int32, (8, obs), 0)
    masks = [(sub + 8 * j) % LOW == low for j in range(3)]
    for i, part in enumerate(parts):
        tiles = []
        for j in range(LANES // 8):
            first, last = 8 * j // LOW, (8 * j + 7) // LOW
            if first >= FIELDS:
                tiles.append(jnp.zeros((8, obs), F32))
                continue
            value = jnp.broadcast_to(part[first : first + 1], (8, obs))
            for f in range(first + 1, last + 1):
                row = part[f : f + 1] if f < FIELDS else 0.0
                value = jnp.where(sub < LOW * f - 8 * j, value, row)
            tiles.append(jnp.where(masks[j % 3], value, 0.0))
        for j in range(0, LANES // 8, 2):
            at = i * LANES + 8 * j
            val_s[at : at + 16, :] = jnp.concatenate(tiles[j : j + 2], 0).astype(BF16)
    code = seg * 8 + high
    for j in range(0, 8 * segs, 64):
        hot_s[j : j + 64, :] = onehot(64, j, code)
    main = nt_dot(hot_s[...], val_s[...])
    main = main[:, :LANES] + main[:, LANES:]
    lane = lax.broadcasted_iota(jnp.int32, (8 * segs, LANES), 1)
    shifted = jnp.concatenate([jnp.zeros((8, LANES), F32), main[:-8]], 0)
    shifted = pltpu.roll(shifted, HALO_LANE, 1)
    out[...] = jnp.where(lane < HALO_LANE, main, shifted).reshape(segs, 8, LANES)


def source_kernel(partials, resid, weight, ids, normal, rhs, left_s):
    obs = ids.shape[0]
    wgt, res, idv = (x[...].reshape(1, obs) for x in (weight, resid, ids))
    count = partials.shape[0]
    part = partials[...]
    rows = [part[p : p + 1] for p in range(count)]
    scaled = part * wgt
    scaled_rows = [scaled[p : p + 1] for p in range(count)]
    terms = [scaled_rows[p] * rows[q] for p, q in SRC_PAIRS]
    terms += [scaled_rows[p] * res for p in range(count)]
    terms += [jnp.zeros((32 - len(terms), obs), F32)]
    high, low = split(jnp.concatenate(terms, 0))
    left_s[0:32, :] = high
    left_s[32:64, :] = low
    left = left_s[...]
    step = 256
    for j in range(0, SRC_DEV, step):
        sums = nt_dot(left, onehot(step, j, idv))
        sums = sums[:32] + sums[32:]
        for t, (p, q) in enumerate(SRC_PAIRS):
            normal[p, q : q + 1, j : j + step] = sums[t : t + 1]
            if p != q:
                normal[q, p : p + 1, j : j + step] = sums[t : t + 1]
        rhs[:, j : j + step] = sums[len(SRC_PAIRS) : len(SRC_PAIRS) + count]


def att_terms(rows, first):
    geoms = rows[:4]
    frac, resid = rows[4], rows[5]
    remain = 1.0 - frac
    square = frac * frac
    cubic = square * frac
    basis = [
        remain * remain * remain * (1.0 / 6.0),
        (3.0 * cubic - 6.0 * square + 4.0) * (1.0 / 6.0),
        (-3.0 * cubic + 3.0 * square + 3.0 * frac + 1.0) * (1.0 / 6.0),
        cubic * (1.0 / 6.0),
    ]
    pairs = [geoms[c] * geoms[e] for c, e in ATT_PAIRS]
    weighted = [geoms[c] * resid for c in range(4)]
    terms = []
    for a in range(first, 4):
        place = GROUP_START[a]
        for c in range(4):
            terms.append((place + c, basis[a] * weighted[c]))
        place = place + 4
        for d in range(4 - a):
            both = basis[a] * basis[a + d]
            for q in range(10):
                terms.append((place + q, both * pairs[q]))
            place = place + 10
        for t in range(place, GROUP_START[a] + GROUP_ROWS[a]):
            terms.append((t, jnp.zeros_like(frac)))
    return terms


def time_kernel(got, out, turned_s, att_f, halo_f, cal_f, att_l, halo_l, cal_l, knot_hot, halo_hot, ccd_hot):
    chunks = got.shape[0] * 8 // LANES
    for c in range(chunks):
        turned_s[c] = got[c * 16 : (c + 1) * 16].reshape(LANES, LANES).T
        rows = [turned_s[c, LOW * f : LOW * f + LOW, :] for f in range(FIELDS + HALO_FIELDS)]
        for t, value in att_terms(rows, 0):
            att_f[c, pl.ds(t, LOW, stride=TERMS), :] = value
        cals = rows[7:13]
        terms = [cals[p] * cals[q] for p, q in CAL_PAIRS]
        terms += [cals[p] * rows[5] for p in range(6)]
        terms += [jnp.zeros((LOW, LANES), F32)] * (32 - len(terms))
        for t, value in enumerate(terms):
            cal_f[c, pl.ds(t, LOW, stride=32), :] = value
        for t, value in att_terms(rows[FIELDS:], 1):
            halo_f[c, pl.ds(t - GROUP_START[1], LOW, stride=EDGE), :] = value
        for l in range(LOW):
            at = (c * LOW + l) * LANES
            cols = slice(at, at + LANES)
            att_l[0:TERMS, cols], att_l[TERMS:, cols] = split(att_f[c, l * TERMS : (l + 1) * TERMS, :])
            halo_l[0:EDGE, cols], halo_l[EDGE:, cols] = split(halo_f[c, l * EDGE : (l + 1) * EDGE, :])
            cal_l[0:32, cols], cal_l[32:, cols] = split(cal_f[c, l * 32 : (l + 1) * 32, :])

            def label(f):
                return turned_s[c, LOW * f + l : LOW * f + l + 1, :].astype(jnp.int32)

            knot_hot[:, cols] = onehot(SEG, 0, label(6))
            ccd_hot[:, cols] = onehot(SEG, 0, label(13))
            halo_hot[:, cols] = onehot(16, SEG - 16, label(FIELDS + 6))
    main = nt_dot(att_l[...], knot_hot[...])
    main = main[:TERMS] + main[TERMS:]
    edge = nt_dot(halo_l[...], halo_hot[...])
    edge = edge[:EDGE] + edge[EDGE:]
    edge = jnp.concatenate([jnp.zeros((EDGE, LANES - 16), F32), edge], 1)
    total = main[: GROUP_ROWS[0]]
    for a in range(1, 4):
        n = GROUP_ROWS[a]
        at = GROUP_START[a]
        group = jnp.concatenate([edge[at - GROUP_START[1] :][:n], main[at : at + n]], 1)
        group = pltpu.roll(group, a, 1)[:, LANES:]
        if n < GROUP_ROWS[0]:
            group = jnp.concatenate([group, jnp.zeros((GROUP_ROWS[0] - n, SEG), F32)], 0)
        total = total + group
    cal = nt_dot(cal_l[...], ccd_hot[...])
    cal = cal[:32] + cal[32:]
    for z in range(out.shape[0]):
        out[z, 0:48, :] = total
        out[z, 48:72, :] = cal[0:24]
        out[z, 44:47, :] = cal[24:27]


def final_kernel(parts, att_normal, att_rhs, cal_normal, cal_rhs, sum_s):
    total = parts[0]
    for z in range(1, parts.shape[0]):
        total = total + parts[z]
    sum_s[...] = total
    att_rhs[...] = sum_s[0:4, :]
    for d in range(4):
        for q, (c, e) in enumerate(ATT_PAIRS):
            row = sum_s[4 + 10 * d + q : 5 + 10 * d + q, :]
            att_normal[d, c, e : e + 1, :] = row
            if c != e:
                att_normal[d, e, c : c + 1, :] = row

    def cal_row(t):
        at = 48 + t if t < 24 else 20 + t
        return sum_s[at : at + 1, :]

    for t, (p, q) in enumerate(CAL_PAIRS):
        cal_normal[p, q : q + 1, :] = cal_row(t)
        if p != q:
            cal_normal[q, p : p + 1, :] = cal_row(t)
    for p in range(6):
        cal_rhs[p : p + 1, :] = cal_row(21 + p)


def call(kernel, out_shape, scratch, vmem_mib, cost, *args, space=pltpu.VMEM):
    return pl.pallas_call(
        kernel,
        out_shape=out_shape,
        in_specs=[pl.BlockSpec(memory_space=space)] * len(args),
        scratch_shapes=scratch,
        compiler_params=pltpu.CompilerParams(vmem_limit_bytes=vmem_mib * 1024 * 1024),
        cost_estimate=pl.CostEstimate(flops=cost, bytes_accessed=200000, transcendentals=0),
    )(*args)


def shape(*dims):
    return jax.ShapeDtypeStruct(dims, F32)


def local(
    src_partials,
    att_geom,
    spline_frac,
    cal_partials,
    residual,
    weight,
    source_ids,
    knot_ids,
    ccd_ids,
):
    obs = residual.shape[0]
    tm_count = lax.axis_size("tm")
    z_count = lax.axis_size("src")
    rows = (att_geom, spline_frac, cal_partials, residual, weight, knot_ids, ccd_ids)
    send = call(
        pack_kernel,
        shape(tm_count, 8, LANES),
        [pltpu.VMEM((8 * tm_count, obs), BF16), pltpu.VMEM((2 * LANES, obs), BF16)]
        + [pltpu.VMEM(x.shape, x.dtype) for x in rows]
        + [pltpu.SemaphoreType.DMA((len(rows),))],
        PACK_MIB,
        1000000000,
        *rows,
        space=pltpu.HBM,
    )
    got = lax.all_to_all(send, "tm", split_axis=0, concat_axis=0, tiled=True)
    src_normal, src_rhs = call(
        source_kernel,
        (shape(5, 5, SRC_DEV), shape(5, SRC_DEV)),
        [pltpu.VMEM((64, obs), BF16)],
        12,
        4000000000,
        src_partials,
        residual,
        weight,
        source_ids,
    )
    got, src_normal, src_rhs = lax.optimization_barrier((got, src_normal, src_rhs))
    chunks = tm_count * 8 // LANES
    depth = chunks * LOW * LANES
    sums = call(
        time_kernel,
        shape(z_count, 72, SEG),
        [
            pltpu.VMEM((chunks, LANES, LANES), F32),
            pltpu.VMEM((chunks, LOW * TERMS, LANES), F32),
            pltpu.VMEM((chunks, LOW * EDGE, LANES), F32),
            pltpu.VMEM((chunks, LOW * 32, LANES), F32),
            pltpu.VMEM((2 * TERMS, depth), BF16),
            pltpu.VMEM((2 * EDGE, depth), BF16),
            pltpu.VMEM((64, depth), BF16),
            pltpu.VMEM((SEG, depth), BF16),
            pltpu.VMEM((16, depth), BF16),
            pltpu.VMEM((SEG, depth), BF16),
        ],
        24,
        1000000000,
        got,
    )
    parts = lax.all_to_all(sums, "src", split_axis=0, concat_axis=0, tiled=True)
    att_normal, att_rhs, cal_normal, cal_rhs = call(
        final_kernel,
        (shape(4, 4, 4, SEG), shape(4, SEG), shape(6, 6, SEG), shape(6, SEG)),
        [pltpu.VMEM((72, SEG), F32)],
        8,
        1000000,
        parts,
    )
    return (src_normal, src_rhs, att_normal, att_rhs, cal_normal, cal_rhs)


def solution(mesh):
    both = ("tm", "src")
    in_specs = (
        P(None, both),
        P(None, both),
        P(both),
        P(None, both),
        P(both),
        P(both),
        P(both),
        P(both),
        P(both),
    )
    out_specs = (
        P(None, None, both),
        P(None, both),
        P(None, None, None, "tm"),
        P(None, "tm"),
        P(None, None, "tm"),
        P(None, "tm"),
    )
    return jax.shard_map(local, mesh=mesh, in_specs=in_specs, out_specs=out_specs, check_vma=False)
```

```python
import jax
import jax.numpy as jnp
from jax import lax
from jax.experimental import pallas as pl
from jax.experimental.pallas import tpu as pltpu
from jax.sharding import PartitionSpec as P

SRC_DEV = 1024
SEG = 256
LANES = 128
F32 = jnp.float32
BF16 = jnp.bfloat16

LOW = 6
FIELDS = 14
HALO_FIELDS = 7
HALO_LANE = LOW * FIELDS
ATT_PAIRS = [(c, e) for c in range(4) for e in range(c, 4)]
CAL_PAIRS = [(p, q) for p in range(6) for q in range(p, 6)]
SRC_PAIRS = [(p, q) for p in range(5) for q in range(p, 5)]
GROUP_ROWS = [48, 40, 24, 16]
GROUP_START = [0, 48, 88, 112]
TERMS = 128
PACK_MIB = 56
EDGE = TERMS - GROUP_START[1]
TERMS_STEP, EDGE_STEP, CAL_STEP = TERMS + 1, EDGE + 1, 32 + 1


def nt_dot(left, right):
    return lax.dot_general(
        left, right, (((1,), (1,)), ((), ())), preferred_element_type=F32
    )


def split(x):
    high = x.astype(BF16)
    return high, (x - high.astype(F32)).astype(BF16)


def onehot(rows, first, ids):
    place = lax.broadcasted_iota(jnp.int32, (rows, ids.shape[1]), 0) + first
    return jnp.where(place == ids, 1.0, 0.0).astype(BF16)


def label_hot(rows, first, ids):
    place = (lax.broadcasted_iota(jnp.int32, (rows, ids.shape[1]), 0) + first).astype(F32).astype(BF16)
    same = place == jnp.broadcast_to(ids, place.shape).astype(BF16)
    return jnp.where(same, jnp.ones_like(place), jnp.zeros_like(place))


def pack_kernel(*refs):
    count = 7
    hot_s, val_s = refs[count + 1 : count + 3]
    out = refs[count]
    held = refs[count + 3 : -1]
    copies = [
        pltpu.make_async_copy(refs[i], held[i], refs[-1].at[i]) for i in range(count)
    ]
    for i in (5, 0, 1, 2, 3, 4, 6):
        copies[i].start()
    geom, frac, cal, resid, weight, knot, ccd = held
    copies[5].wait()
    obs = knot.shape[0]
    segs = out.shape[0]
    chunk = 256
    blocks = obs // chunk
    knots = knot[...].reshape(1, obs)
    seg = knots // SEG
    member = label_hot(segs, 0, seg.astype(F32))
    before = lax.broadcasted_iota(jnp.int32, (chunk, chunk), 0) < lax.broadcasted_iota(
        jnp.int32, (chunk, chunk), 1
    )
    before = jnp.where(before, 1.0, 0.0).astype(BF16)
    counter = jnp.concatenate([before, jnp.ones((chunk, LANES), BF16)], 1)
    carry = jnp.zeros((segs, LANES), F32)
    ranks = []
    for b in range(blocks):
        here = member[:, b * chunk : (b + 1) * chunk]
        counts = jnp.dot(here, counter, preferred_element_type=F32)
        for half in range(chunk // LANES):
            cols = slice(half * LANES, (half + 1) * LANES)
            ranks.append(
                jnp.sum(here[:, cols].astype(F32) * (counts[:, cols] + carry), 0, keepdims=True)
            )
        carry = carry + counts[:, chunk:]
    rank = jnp.concatenate(ranks, 1).astype(jnp.int32)
    high = (rank * 43) >> 8
    low = rank - LOW * high

    for i in (0, 1, 2, 3, 4, 6):
        copies[i].wait()
    scale = jnp.sqrt(weight[...].reshape(1, obs))
    geoms = geom[...] * scale
    cals = cal[...] * scale
    fields = [geoms[c : c + 1] for c in range(4)]
    fields += [frac[...].reshape(1, obs), resid[...].reshape(1, obs) * scale]
    fields += [(knots - SEG * seg).astype(F32)]
    fields += [cals[p : p + 1] for p in range(6)]
    fields += [ccd[...].reshape(1, obs).astype(F32)]
    fields = jnp.concatenate(fields, 0)
    rounded = fields.astype(BF16).astype(F32)
    parts = (rounded, fields - rounded)
    sub = lax.broadcasted_iota(jnp.int32, (8, obs), 0)
    masks = [(sub + 8 * j) % LOW == low for j in range(3)]
    for i, part in enumerate(parts):
        tiles = []
        for j in range(LANES // 8):
            first, last = 8 * j // LOW, (8 * j + 7) // LOW
            if first >= FIELDS:
                tiles.append(jnp.zeros((8, obs), F32))
                continue
            value = jnp.broadcast_to(part[first : first + 1], (8, obs))
            for f in range(first + 1, last + 1):
                row = part[f : f + 1] if f < FIELDS else 0.0
                value = jnp.where(sub < LOW * f - 8 * j, value, row)
            tiles.append(jnp.where(masks[j % 3], value, 0.0))
        for j in range(0, LANES // 8, 2):
            at = i * LANES + 8 * j
            val_s[at : at + 16, :] = jnp.concatenate(tiles[j : j + 2], 0).astype(BF16)
    code = seg * 8 + high
    for j in range(0, 8 * segs, 64):
        hot_s[j : j + 64, :] = label_hot(64, 0, (code - j).astype(F32))
    main = nt_dot(hot_s[...], val_s[...])
    main = main[:, :LANES] + main[:, LANES:]
    lane = lax.broadcasted_iota(jnp.int32, (8 * segs, LANES), 1)
    shifted = jnp.concatenate([jnp.zeros((8, LANES), F32), main[:-8]], 0)
    shifted = pltpu.roll(shifted, HALO_LANE, 1)
    out[...] = jnp.where(lane < HALO_LANE, main, shifted).reshape(segs, 8, LANES)


def source_kernel(partials, resid, weight, ids, normal, rhs, left_s):
    obs = ids.shape[0]
    wgt, res, idv = (x[...].reshape(1, obs) for x in (weight, resid, ids))
    count = partials.shape[0]
    part = partials[...]
    rows = [part[p : p + 1] for p in range(count)]
    scaled = part * wgt
    scaled_rows = [scaled[p : p + 1] for p in range(count)]
    terms = [scaled_rows[p] * rows[q] for p, q in SRC_PAIRS]
    terms += [scaled_rows[p] * res for p in range(count)]
    terms += [jnp.zeros((32 - len(terms), obs), F32)]
    high, low = split(jnp.concatenate(terms, 0))
    left_s[0:32, :] = high
    left_s[32:64, :] = low
    left = left_s[...]
    step = 256
    for j in range(0, SRC_DEV, step):
        sums = nt_dot(left, onehot(step, j, idv))
        sums = sums[:32] + sums[32:]
        for t, (p, q) in enumerate(SRC_PAIRS):
            normal[p, q : q + 1, j : j + step] = sums[t : t + 1]
            if p != q:
                normal[q, p : p + 1, j : j + step] = sums[t : t + 1]
        rhs[:, j : j + step] = sums[len(SRC_PAIRS) : len(SRC_PAIRS) + count]


def att_terms(rows, first):
    geoms = rows[:4]
    frac, resid = rows[4], rows[5]
    remain = 1.0 - frac
    square = frac * frac
    cubic = square * frac
    basis = [
        remain * remain * remain * (1.0 / 6.0),
        (3.0 * cubic - 6.0 * square + 4.0) * (1.0 / 6.0),
        (-3.0 * cubic + 3.0 * square + 3.0 * frac + 1.0) * (1.0 / 6.0),
        cubic * (1.0 / 6.0),
    ]
    pairs = [geoms[c] * geoms[e] for c, e in ATT_PAIRS]
    weighted = [geoms[c] * resid for c in range(4)]
    terms = []
    for a in range(first, 4):
        place = GROUP_START[a]
        for c in range(4):
            terms.append((place + c, basis[a] * weighted[c]))
        place = place + 4
        for d in range(4 - a):
            both = basis[a] * basis[a + d]
            for q in range(10):
                terms.append((place + q, both * pairs[q]))
            place = place + 10
        for t in range(place, GROUP_START[a] + GROUP_ROWS[a]):
            terms.append((t, jnp.zeros_like(frac)))
    return terms


def time_kernel(got, out, turned_s, att_f, halo_f, cal_f, att_l, halo_l, cal_l, knot_hot, halo_hot, ccd_hot):
    chunks = got.shape[0] * 8 // LANES
    for c in range(chunks):
        turned_s[c] = got[c * 16 : (c + 1) * 16].reshape(LANES, LANES).T
        rows = [turned_s[c, LOW * f : LOW * f + LOW, :] for f in range(FIELDS + HALO_FIELDS)]
        for t, value in att_terms(rows, 0):
            att_f[c, pl.ds(t, LOW, stride=TERMS_STEP), :] = value
        cals = rows[7:13]
        terms = [cals[p] * cals[q] for p, q in CAL_PAIRS]
        terms += [cals[p] * rows[5] for p in range(6)]
        terms += [jnp.zeros((LOW, LANES), F32)] * (32 - len(terms))
        for t, value in enumerate(terms):
            cal_f[c, pl.ds(t, LOW, stride=CAL_STEP), :] = value
        for t, value in att_terms(rows[FIELDS:], 1):
            halo_f[c, pl.ds(t - GROUP_START[1], LOW, stride=EDGE_STEP), :] = value
        for l in range(LOW):
            at = l * LANES
            cols = slice(at, at + LANES)
            att_l[c, 0:TERMS, cols], att_l[c, TERMS:, cols] = split(att_f[c, l * TERMS_STEP : l * TERMS_STEP + TERMS, :])
            halo_l[c, 0:EDGE, cols], halo_l[c, EDGE:, cols] = split(halo_f[c, l * EDGE_STEP : l * EDGE_STEP + EDGE, :])
            cal_l[c, 0:32, cols], cal_l[c, 32:, cols] = split(cal_f[c, l * CAL_STEP : l * CAL_STEP + 32, :])

            def label(f):
                return turned_s[c, LOW * f + l : LOW * f + l + 1, :]

            knot_hot[c, :, cols] = label_hot(SEG, 0, label(6))
            ccd_hot[c, :, cols] = label_hot(SEG, 0, label(13))
            halo_hot[c, :, cols] = label_hot(16, SEG - 16, label(FIELDS + 6))
        sums = (
            nt_dot(att_l[c], knot_hot[c]),
            nt_dot(halo_l[c], halo_hot[c]),
            nt_dot(cal_l[c], ccd_hot[c]),
        )
        totals = sums if c == 0 else tuple(x + y for x, y in zip(totals, sums))
    main, edge, cal = totals
    main = main[:TERMS] + main[TERMS:]
    edge = edge[:EDGE] + edge[EDGE:]
    edge = jnp.concatenate([jnp.zeros((EDGE, LANES - 16), F32), edge], 1)
    total = main[: GROUP_ROWS[0]]
    for a in range(1, 4):
        n = GROUP_ROWS[a]
        at = GROUP_START[a]
        group = jnp.concatenate([edge[at - GROUP_START[1] :][:n], main[at : at + n]], 1)
        group = pltpu.roll(group, a, 1)[:, LANES:]
        if n < GROUP_ROWS[0]:
            group = jnp.concatenate([group, jnp.zeros((GROUP_ROWS[0] - n, SEG), F32)], 0)
        total = total + group
    cal = cal[:32] + cal[32:]
    for z in range(out.shape[0]):
        out[z, 0:48, :] = total
        out[z, 48:72, :] = cal[0:24]
        out[z, 44:47, :] = cal[24:27]


def final_kernel(parts, att_normal, att_rhs, cal_normal, cal_rhs, sum_s):
    total = parts[0]
    for z in range(1, parts.shape[0]):
        total = total + parts[z]
    sum_s[...] = total
    att_rhs[...] = sum_s[0:4, :]
    for d in range(4):
        for q, (c, e) in enumerate(ATT_PAIRS):
            row = sum_s[4 + 10 * d + q : 5 + 10 * d + q, :]
            att_normal[d, c, e : e + 1, :] = row
            if c != e:
                att_normal[d, e, c : c + 1, :] = row

    def cal_row(t):
        at = 48 + t if t < 24 else 20 + t
        return sum_s[at : at + 1, :]

    for t, (p, q) in enumerate(CAL_PAIRS):
        cal_normal[p, q : q + 1, :] = cal_row(t)
        if p != q:
            cal_normal[q, p : p + 1, :] = cal_row(t)
    for p in range(6):
        cal_rhs[p : p + 1, :] = cal_row(21 + p)


def call(kernel, out_shape, scratch, vmem_mib, cost, *args, space=pltpu.VMEM):
    return pl.pallas_call(
        kernel,
        out_shape=out_shape,
        in_specs=[pl.BlockSpec(memory_space=space)] * len(args),
        scratch_shapes=scratch,
        compiler_params=pltpu.CompilerParams(vmem_limit_bytes=vmem_mib * 1024 * 1024),
        cost_estimate=pl.CostEstimate(flops=cost, bytes_accessed=200000, transcendentals=0),
    )(*args)


def shape(*dims):
    return jax.ShapeDtypeStruct(dims, F32)


def local(
    src_partials,
    att_geom,
    spline_frac,
    cal_partials,
    residual,
    weight,
    source_ids,
    knot_ids,
    ccd_ids,
):
    obs = residual.shape[0]
    tm_count = lax.axis_size("tm")
    z_count = lax.axis_size("src")
    rows = (att_geom, spline_frac, cal_partials, residual, weight, knot_ids, ccd_ids)
    send = call(
        pack_kernel,
        shape(tm_count, 8, LANES),
        [pltpu.VMEM((8 * tm_count, obs), BF16), pltpu.VMEM((2 * LANES, obs), BF16)]
        + [pltpu.VMEM(x.shape, x.dtype) for x in rows]
        + [pltpu.SemaphoreType.DMA((len(rows),))],
        PACK_MIB,
        1000000000,
        *rows,
        space=pltpu.HBM,
    )
    got = lax.all_to_all(send, "tm", split_axis=0, concat_axis=0, tiled=True)
    src_normal, src_rhs = call(
        source_kernel,
        (shape(5, 5, SRC_DEV), shape(5, SRC_DEV)),
        [pltpu.VMEM((64, obs), BF16)],
        12,
        4000000000,
        src_partials,
        residual,
        weight,
        source_ids,
    )
    got, src_normal, src_rhs = lax.optimization_barrier((got, src_normal, src_rhs))
    chunks = tm_count * 8 // LANES
    depth = LOW * LANES
    sums = call(
        time_kernel,
        shape(z_count, 72, SEG),
        [
            pltpu.VMEM((chunks, LANES, LANES), F32),
            pltpu.VMEM((chunks, 8 * TERMS_STEP, LANES), F32),
            pltpu.VMEM((chunks, 8 * EDGE_STEP, LANES), F32),
            pltpu.VMEM((chunks, 8 * CAL_STEP, LANES), F32),
            pltpu.VMEM((chunks, 2 * TERMS, depth), BF16),
            pltpu.VMEM((chunks, 2 * EDGE, depth), BF16),
            pltpu.VMEM((chunks, 64, depth), BF16),
            pltpu.VMEM((chunks, SEG, depth), BF16),
            pltpu.VMEM((chunks, 16, depth), BF16),
            pltpu.VMEM((chunks, SEG, depth), BF16),
        ],
        24,
        1000000000,
        got,
    )
    parts = lax.all_to_all(sums, "src", split_axis=0, concat_axis=0, tiled=True)
    att_normal, att_rhs, cal_normal, cal_rhs = call(
        final_kernel,
        (shape(4, 4, 4, SEG), shape(4, SEG), shape(6, 6, SEG), shape(6, SEG)),
        [pltpu.VMEM((72, SEG), F32)],
        8,
        1000000,
        parts,
    )
    return (src_normal, src_rhs, att_normal, att_rhs, cal_normal, cal_rhs)


def solution(mesh):
    both = ("tm", "src")
    in_specs = (
        P(None, both),
        P(None, both),
        P(both),
        P(None, both),
        P(both),
        P(both),
        P(both),
        P(both),
        P(both),
    )
    out_specs = (
        P(None, None, both),
        P(None, both),
        P(None, None, None, "tm"),
        P(None, "tm"),
        P(None, None, "tm"),
        P(None, "tm"),
    )
    return jax.shard_map(local, mesh=mesh, in_specs=in_specs, out_specs=out_specs, check_vma=False)
```

```python
import jax
import jax.numpy as jnp
from jax import lax
from jax.experimental import pallas as pl
from jax.experimental.pallas import tpu as pltpu
from jax.sharding import PartitionSpec as P

SRC_DEV = 1024
SEG = 256
LANES = 128
F32 = jnp.float32
BF16 = jnp.bfloat16

LOW = 8
HIGH = 6
FIELDS = 14
SPILL = [(0, 0), (1, 0), (2, 0), (0, 1), (1, 1), (0, 2)]
SPILL_LANE = LOW * FIELDS
ATT_PAIRS = [(c, e) for c in range(4) for e in range(c, 4)]
CAL_PAIRS = [(p, q) for p in range(6) for q in range(p, 6)]
SRC_PAIRS = [(p, q) for p in range(5) for q in range(p, 5)]
GROUP_ROWS = [48, 40, 24, 16]
GROUP_START = [0, 48, 88, 112]
TERMS = 128
PACK_MIB = 56
TERMS_STEP, CAL_STEP = TERMS + 1, 32 + 1


def nt_dot(left, right):
    return lax.dot_general(
        left, right, (((1,), (1,)), ((), ())), preferred_element_type=F32
    )


def split(x):
    high = x.astype(BF16)
    return high, (x - high.astype(F32)).astype(BF16)


def onehot(rows, first, ids):
    place = lax.broadcasted_iota(jnp.int32, (rows, ids.shape[1]), 0) + first
    return jnp.where(place == ids, 1.0, 0.0).astype(BF16)


def label_hot(rows, first, ids):
    place = (lax.broadcasted_iota(jnp.int32, (rows, ids.shape[1]), 0) + first).astype(F32).astype(BF16)
    same = place == jnp.broadcast_to(ids, place.shape).astype(BF16)
    return jnp.where(same, jnp.ones_like(place), jnp.zeros_like(place))


def pack_kernel(*refs):
    count = 7
    out = refs[count]
    hot_s, val_s, spill_s, tile_s = refs[count + 1 : count + 5]
    held = refs[count + 5 : -1]
    copies = [
        pltpu.make_async_copy(refs[i], held[i], refs[-1].at[i]) for i in range(count)
    ]
    for i in (5, 0, 1, 2, 3, 4, 6):
        copies[i].start()
    geom, frac, cal, resid, weight, knot, ccd = held
    copies[5].wait()
    obs = knot.shape[0]
    segs = out.shape[0]
    chunk = 256
    blocks = obs // chunk
    knots = knot[...].reshape(1, obs)
    seg = knots // SEG
    member = label_hot(segs, 0, seg.astype(F32))
    before = lax.broadcasted_iota(jnp.int32, (chunk, chunk), 0) < lax.broadcasted_iota(
        jnp.int32, (chunk, chunk), 1
    )
    before = jnp.where(before, 1.0, 0.0).astype(BF16)
    counter = jnp.concatenate([before, jnp.ones((chunk, LANES), BF16)], 1)
    carry = jnp.zeros((segs, LANES), F32)
    ranks = []
    for b in range(blocks):
        here = member[:, b * chunk : (b + 1) * chunk]
        counts = jnp.dot(here, counter, preferred_element_type=F32)
        for half in range(chunk // LANES):
            cols = slice(half * LANES, (half + 1) * LANES)
            ranks.append(
                jnp.sum(here[:, cols].astype(F32) * (counts[:, cols] + carry), 0, keepdims=True)
            )
        carry = carry + counts[:, chunk:]
    rank = jnp.concatenate(ranks, 1).astype(jnp.int32)
    high = rank >> 3
    low = rank & 7

    for i in (0, 1, 2, 3, 4, 6):
        copies[i].wait()
    scale = jnp.sqrt(weight[...].reshape(1, obs))
    geoms = geom[...] * scale
    cals = cal[...] * scale
    place = knots - SEG * seg
    frac_row = frac[...].reshape(1, obs)
    geom_rows = [geoms[c : c + 1] for c in range(4)]
    resid_row = resid[...].reshape(1, obs) * scale
    fields = geom_rows + [frac_row, resid_row, place.astype(F32)]
    fields += [cals[p : p + 1] for p in range(6)]
    fields += [ccd[...].reshape(1, obs).astype(F32)]

    basis = spline_basis(frac_row)
    spill = []
    for j in range(3):
        value = jnp.zeros_like(frac_row)
        for a in range(j + 1, 4):
            value = jnp.where(place == SEG + j - a, basis[a], value)
        spill.append(value)
    left = [geom_rows[c] for c, _ in ATT_PAIRS] + [resid_row] * 4
    right = [geom_rows[e] for _, e in ATT_PAIRS] + geom_rows
    zero = jnp.zeros((1, obs), F32)
    both = [
        jnp.concatenate(left[at : at + 8] + [zero] * max(0, at + 8 - 14), 0)
        * jnp.concatenate(right[at : at + 8] + [zero] * max(0, at + 8 - 14), 0)
        for at in (0, 8)
    ]
    sub = lax.broadcasted_iota(jnp.int32, (8, obs), 0)
    for s, (j, d) in enumerate(SPILL):
        pair = spill[j] * spill[j + d]
        other = spill[j] if d == 0 else zero
        terms = [both[0] * pair, both[1] * jnp.where(sub < 2, pair, other)]
        top, rest = split(jnp.concatenate(terms, 0))
        spill_s[16 * s : 16 * s + 16, :] = top
        spill_s[LANES + 16 * s : LANES + 16 * s + 16, :] = rest
    for at in (16 * HIGH, LANES + 16 * HIGH):
        spill_s[at : at + LANES - 16 * HIGH, :] = jnp.zeros((LANES - 16 * HIGH, obs), BF16)

    fields = jnp.concatenate(fields, 0)
    rounded = fields.astype(BF16).astype(F32)
    low_is = sub == low
    for i, part in enumerate((rounded, fields - rounded)):
        for f in range(0, FIELDS, 2):
            pair = [jnp.where(low_is, part[f + n : f + n + 1], 0.0) for n in range(2)]
            at = i * LANES + LOW * f
            val_s[at : at + 16, :] = jnp.concatenate(pair, 0).astype(BF16)
        val_s[i * LANES + SPILL_LANE : (i + 1) * LANES, :] = jnp.zeros((16, obs), BF16)
    code = (high >> 1) * (2 * segs) + 2 * seg + (high & 1)
    for j in range(0, HIGH * segs, 64):
        hot_s[j : j + 64, :] = label_hot(64, 0, (code - j).astype(F32))
    main = nt_dot(hot_s[...], val_s[...])
    main = main[:, :LANES] + main[:, LANES:]
    row = lax.broadcasted_iota(jnp.int32, (2 * segs, obs), 0) >> 1
    sums = nt_dot(jnp.where(row == seg + 1, 1.0, 0.0).astype(BF16), spill_s[...])
    sums = sums[:, :LANES] + sums[:, LANES:]
    lane = lax.broadcasted_iota(jnp.int32, (2 * segs, LANES), 1)
    even = lax.broadcasted_iota(jnp.int32, (2 * segs, LANES), 0) & 1 == 0
    for m in range(HIGH // 2):
        edge = jnp.where(
            even,
            pltpu.roll(sums, SPILL_LANE - 32 * m, 1),
            pltpu.roll(sums, SPILL_LANE - 32 * m - 16, 1),
        )
        tile_s[m] = jnp.where(lane < SPILL_LANE, main[2 * segs * m : 2 * segs * (m + 1)], edge)
        for t in range(segs):
            out[t, :, m * LANES : (m + 1) * LANES] = tile_s[m, 2 * t : 2 * t + 2, :]


def source_kernel(partials, resid, weight, ids, normal, rhs, left_s):
    obs = ids.shape[0]
    wgt, res, idv = (x[...].reshape(1, obs) for x in (weight, resid, ids))
    count = partials.shape[0]
    part = partials[...]
    rows = [part[p : p + 1] for p in range(count)]
    scaled = part * wgt
    scaled_rows = [scaled[p : p + 1] for p in range(count)]
    terms = [scaled_rows[p] * rows[q] for p, q in SRC_PAIRS]
    terms += [scaled_rows[p] * res for p in range(count)]
    terms += [jnp.zeros((32 - len(terms), obs), F32)]
    high, low = split(jnp.concatenate(terms, 0))
    left_s[0:32, :] = high
    left_s[32:64, :] = low
    left = left_s[...]
    step = 256
    for j in range(0, SRC_DEV, step):
        sums = nt_dot(left, onehot(step, j, idv))
        sums = sums[:32] + sums[32:]
        for t, (p, q) in enumerate(SRC_PAIRS):
            normal[p, q : q + 1, j : j + step] = sums[t : t + 1]
            if p != q:
                normal[q, p : p + 1, j : j + step] = sums[t : t + 1]
        rhs[:, j : j + step] = sums[len(SRC_PAIRS) : len(SRC_PAIRS) + count]


def spline_basis(frac):
    remain = 1.0 - frac
    square = frac * frac
    cubic = square * frac
    return [
        remain * remain * remain * (1.0 / 6.0),
        (3.0 * cubic - 6.0 * square + 4.0) * (1.0 / 6.0),
        (-3.0 * cubic + 3.0 * square + 3.0 * frac + 1.0) * (1.0 / 6.0),
        cubic * (1.0 / 6.0),
    ]


def att_terms(rows):
    geoms, frac, resid = rows[:4], rows[4], rows[5]
    basis = spline_basis(frac)
    pairs = [geoms[c] * geoms[e] for c, e in ATT_PAIRS]
    weighted = [geoms[c] * resid for c in range(4)]
    terms = []
    for a in range(4):
        place = GROUP_START[a]
        for c in range(4):
            terms.append((place + c, basis[a] * weighted[c]))
        place = place + 4
        for d in range(4 - a):
            both = basis[a] * basis[a + d]
            for q in range(10):
                terms.append((place + q, both * pairs[q]))
            place = place + 10
        for t in range(place, GROUP_START[a] + GROUP_ROWS[a]):
            terms.append((t, jnp.zeros_like(frac)))
    return terms


def time_kernel(got, out, tile_s, turned_s, att_f, cal_f, att_l, cal_l, knot_hot, ccd_hot, edge_s, sum_s):
    segs = got.shape[0]
    columns = []
    parity = lax.broadcasted_iota(jnp.int32, (16, LANES), 1) & 1
    for c in range(HIGH // 2):
        for t in range(segs):
            tile_s[c, 2 * t : 2 * t + 2, :] = got[t, :, c * LANES : (c + 1) * LANES]
        turned_s[c] = tile_s[c].T
        edge = turned_s[c, SPILL_LANE:, :]
        for r in range(2):
            columns.append(jnp.sum(jnp.where(parity == r, edge, 0.0), 1, keepdims=True))
        rows = [turned_s[c, LOW * f : LOW * f + LOW, :] for f in range(FIELDS)]
        for t, value in att_terms(rows):
            att_f[c, pl.ds(t, LOW, stride=TERMS_STEP), :] = value
        cals = rows[7:13]
        terms = [cals[p] * cals[q] for p, q in CAL_PAIRS]
        terms += [cals[p] * rows[5] for p in range(6)]
        terms += [jnp.zeros((LOW, LANES), F32)] * (32 - len(terms))
        for t, value in enumerate(terms):
            cal_f[c, pl.ds(t, LOW, stride=CAL_STEP), :] = value
        for l in range(LOW):
            cols = slice(l * LANES, (l + 1) * LANES)
            att_l[c, 0:TERMS, cols], att_l[c, TERMS:, cols] = split(
                att_f[c, l * TERMS_STEP : l * TERMS_STEP + TERMS, :]
            )
            cal_l[c, 0:32, cols], cal_l[c, 32:, cols] = split(
                cal_f[c, l * CAL_STEP : l * CAL_STEP + 32, :]
            )
            for hot, f in ((knot_hot, 6), (ccd_hot, 13)):
                at = LOW * f + l
                hot[c, :, cols] = label_hot(SEG, 0, turned_s[c, at : at + 1, :])
        sums = (nt_dot(att_l[c], knot_hot[c]), nt_dot(cal_l[c], ccd_hot[c]))
        totals = sums if c == 0 else tuple(x + y for x, y in zip(totals, sums))
    main, cal = totals
    main = main[:TERMS] + main[TERMS:]
    cal = cal[:32] + cal[32:]
    lane = lax.broadcasted_iota(jnp.int32, (16, LANES), 1)
    edge_s[...] = jnp.zeros(edge_s.shape, F32)
    for d in range(3):
        block = jnp.zeros((16, LANES), F32)
        for s, (j, gap) in enumerate(SPILL):
            if gap == d:
                block = jnp.where(lane == j, columns[s], block)
        edge_s[4 + 10 * d : 14 + 10 * d, :] = block[0:10]
        if d == 0:
            edge_s[0:4, :] = block[10:14]
    total = main[: GROUP_ROWS[0]]
    for a in range(1, 4):
        n = GROUP_ROWS[a]
        group = pltpu.roll(main[GROUP_START[a] : GROUP_START[a] + n], a, 1)
        group = jnp.where(lax.broadcasted_iota(jnp.int32, (n, SEG), 1) < a, 0.0, group)
        if n < GROUP_ROWS[0]:
            group = jnp.concatenate([group, jnp.zeros((GROUP_ROWS[0] - n, SEG), F32)], 0)
        total = total + group
    for h in range(2):
        cols = slice(h * LANES, (h + 1) * LANES)
        sum_s[72 * h : 72 * h + 48, :] = total[:, cols] + edge_s[...] if h == 0 else total[:, cols]
        sum_s[72 * h + 48 : 72 * h + 72, :] = cal[0:24, cols]
        sum_s[72 * h + 44 : 72 * h + 47, :] = cal[24:27, cols]
    for z in range(out.shape[0]):
        for j in range(9):
            at = 18 * z + 2 * j
            out[z, :, j * LANES : (j + 1) * LANES] = sum_s[at : at + 2, :]


def middle_kernel(parts, out):
    total = parts[0]
    for z in range(1, parts.shape[0]):
        total = total + parts[z]
    for z in range(out.shape[0]):
        out[z] = total


def final_kernel(parts, att_normal, att_rhs, cal_normal, cal_rhs, sum_s):
    for z in range(parts.shape[0]):
        for j in range(9):
            half, at = divmod(18 * z + 2 * j, 72)
            cols = slice(half * LANES, (half + 1) * LANES)
            sum_s[at : at + 2, cols] = parts[z, :, j * LANES : (j + 1) * LANES]
    att_rhs[...] = sum_s[0:4, :]
    for d in range(4):
        for q, (c, e) in enumerate(ATT_PAIRS):
            row = sum_s[4 + 10 * d + q : 5 + 10 * d + q, :]
            att_normal[d, c, e : e + 1, :] = row
            if c != e:
                att_normal[d, e, c : c + 1, :] = row

    def cal_row(t):
        at = 48 + t if t < 24 else 20 + t
        return sum_s[at : at + 1, :]

    for t, (p, q) in enumerate(CAL_PAIRS):
        cal_normal[p, q : q + 1, :] = cal_row(t)
        if p != q:
            cal_normal[q, p : p + 1, :] = cal_row(t)
    for p in range(6):
        cal_rhs[p : p + 1, :] = cal_row(21 + p)


def call(kernel, out_shape, scratch, vmem_mib, cost, *args, space=pltpu.VMEM):
    return pl.pallas_call(
        kernel,
        out_shape=out_shape,
        in_specs=[pl.BlockSpec(memory_space=space)] * len(args),
        scratch_shapes=scratch,
        compiler_params=pltpu.CompilerParams(vmem_limit_bytes=vmem_mib * 1024 * 1024),
        cost_estimate=pl.CostEstimate(flops=cost, bytes_accessed=200000, transcendentals=0),
    )(*args)


def shape(*dims):
    return jax.ShapeDtypeStruct(dims, F32)


def local(
    src_partials,
    att_geom,
    spline_frac,
    cal_partials,
    residual,
    weight,
    source_ids,
    knot_ids,
    ccd_ids,
):
    obs = residual.shape[0]
    tm_count = lax.axis_size("tm")
    z_count = lax.axis_size("src")
    rows = (att_geom, spline_frac, cal_partials, residual, weight, knot_ids, ccd_ids)
    send = call(
        pack_kernel,
        shape(tm_count, 2, HIGH // 2 * LANES),
        [
            pltpu.VMEM((HIGH * tm_count, obs), BF16),
            pltpu.VMEM((2 * LANES, obs), BF16),
            pltpu.VMEM((2 * LANES, obs), BF16),
            pltpu.VMEM((HIGH // 2, 2 * tm_count, LANES), F32),
        ]
        + [pltpu.VMEM(x.shape, x.dtype) for x in rows]
        + [pltpu.SemaphoreType.DMA((len(rows),))],
        PACK_MIB,
        1000000000,
        *rows,
        space=pltpu.HBM,
    )
    got = lax.all_to_all(send, "tm", split_axis=0, concat_axis=0, tiled=True)
    src_normal, src_rhs = call(
        source_kernel,
        (shape(5, 5, SRC_DEV), shape(5, SRC_DEV)),
        [pltpu.VMEM((64, obs), BF16)],
        12,
        4000000000,
        src_partials,
        residual,
        weight,
        source_ids,
    )
    got, src_normal, src_rhs = lax.optimization_barrier((got, src_normal, src_rhs))
    chunks = HIGH // 2
    depth = LOW * LANES
    sums = call(
        time_kernel,
        shape(z_count, 2, 9 * LANES),
        [
            pltpu.VMEM((chunks, 2 * tm_count, LANES), F32),
            pltpu.VMEM((chunks, LANES, LANES), F32),
            pltpu.VMEM((chunks, LOW * TERMS_STEP, LANES), F32),
            pltpu.VMEM((chunks, LOW * CAL_STEP, LANES), F32),
            pltpu.VMEM((chunks, 2 * TERMS, depth), BF16),
            pltpu.VMEM((chunks, 64, depth), BF16),
            pltpu.VMEM((chunks, SEG, depth), BF16),
            pltpu.VMEM((chunks, SEG, depth), BF16),
            pltpu.VMEM((48, LANES), F32),
            pltpu.VMEM((144, LANES), F32),
        ],
        24,
        1000000000,
        got,
    )
    parts = lax.all_to_all(sums, "src", split_axis=0, concat_axis=0, tiled=True)
    parts = call(middle_kernel, shape(z_count, 2, 9 * LANES), [], 8, 1000000, parts)
    parts = lax.all_to_all(parts, "src", split_axis=0, concat_axis=0, tiled=True)
    att_normal, att_rhs, cal_normal, cal_rhs = call(
        final_kernel,
        (shape(4, 4, 4, SEG), shape(4, SEG), shape(6, 6, SEG), shape(6, SEG)),
        [pltpu.VMEM((72, SEG), F32)],
        8,
        1000000,
        parts,
    )
    return (src_normal, src_rhs, att_normal, att_rhs, cal_normal, cal_rhs)


def solution(mesh):
    both = ("tm", "src")
    in_specs = (
        P(None, both),
        P(None, both),
        P(both),
        P(None, both),
        P(both),
        P(both),
        P(both),
        P(both),
        P(both),
    )
    out_specs = (
        P(None, None, both),
        P(None, both),
        P(None, None, None, "tm"),
        P(None, "tm"),
        P(None, None, "tm"),
        P(None, "tm"),
    )
    return jax.shard_map(local, mesh=mesh, in_specs=in_specs, out_specs=out_specs, check_vma=False)
```

```python
import jax
import jax.numpy as jnp
from jax import lax
from jax.experimental import pallas as pl
from jax.experimental.pallas import tpu as pltpu
from jax.sharding import PartitionSpec as P

SRC_DEV = 1024
SEG = 256
LANES = 128
F32 = jnp.float32
BF16 = jnp.bfloat16

LOW = 8
HIGH = 6
FIELDS = 14
SPILL = [(0, 0), (1, 0), (2, 0), (0, 1), (1, 1), (0, 2)]
SPILL_LANE = LOW * FIELDS
ATT_PAIRS = [(c, e) for c in range(4) for e in range(c, 4)]
CAL_PAIRS = [(p, q) for p in range(6) for q in range(p, 6)]
SRC_PAIRS = [(p, q) for p in range(5) for q in range(p, 5)]
GROUP_ROWS = [48, 40, 24, 16]
GROUP_START = [0, 48, 88, 112]
TERMS = 128
PACK_MIB = 56
TERMS_STEP, CAL_STEP = TERMS + 1, 32 + 1


def nt_dot(left, right):
    return lax.dot_general(
        left, right, (((1,), (1,)), ((), ())), preferred_element_type=F32
    )


def split(x):
    high = x.astype(BF16)
    return high, (x - high.astype(F32)).astype(BF16)


def onehot(rows, first, ids):
    place = lax.broadcasted_iota(jnp.int32, (rows, ids.shape[1]), 0) + first
    return jnp.where(place == ids, 1.0, 0.0).astype(BF16)


def label_hot(rows, first, ids):
    place = (lax.broadcasted_iota(jnp.int32, (rows, ids.shape[1]), 0) + first).astype(F32).astype(BF16)
    same = place == jnp.broadcast_to(ids, place.shape).astype(BF16)
    return jnp.where(same, jnp.ones_like(place), jnp.zeros_like(place))


def pack_kernel(*refs):
    count = 7
    out = refs[count]
    hot_s, val_s, spill_s, tile_s = refs[count + 1 : count + 5]
    held = refs[count + 5 : -1]
    copies = [
        pltpu.make_async_copy(refs[i], held[i], refs[-1].at[i]) for i in range(count)
    ]
    for i in (5, 0, 1, 2, 3, 4, 6):
        copies[i].start()
    geom, frac, cal, resid, weight, knot, ccd = held
    copies[5].wait()
    obs = knot.shape[0]
    segs = out.shape[0]
    chunk = 256
    blocks = obs // chunk
    knots = knot[...].reshape(1, obs)
    seg = knots // SEG
    member = label_hot(segs, 0, seg.astype(F32))
    before = lax.broadcasted_iota(jnp.int32, (chunk, chunk), 0) < lax.broadcasted_iota(
        jnp.int32, (chunk, chunk), 1
    )
    before = jnp.where(before, 1.0, 0.0).astype(BF16)
    counter = jnp.concatenate([before, jnp.ones((chunk, LANES), BF16)], 1)
    carry = jnp.zeros((segs, LANES), F32)
    ranks = []
    for b in range(blocks):
        here = member[:, b * chunk : (b + 1) * chunk]
        counts = jnp.dot(here, counter, preferred_element_type=F32)
        for half in range(chunk // LANES):
            cols = slice(half * LANES, (half + 1) * LANES)
            ranks.append(
                jnp.sum(here[:, cols].astype(F32) * (counts[:, cols] + carry), 0, keepdims=True)
            )
        carry = carry + counts[:, chunk:]
    rank = jnp.concatenate(ranks, 1).astype(jnp.int32)
    high = rank >> 3
    low = rank & 7

    for i in (0, 1, 2, 3, 4, 6):
        copies[i].wait()
    scale = jnp.sqrt(weight[...].reshape(1, obs))
    geoms = geom[...] * scale
    cals = cal[...] * scale
    place = knots - SEG * seg
    frac_row = frac[...].reshape(1, obs)
    geom_rows = [geoms[c : c + 1] for c in range(4)]
    resid_row = resid[...].reshape(1, obs) * scale
    fields = geom_rows + [frac_row, resid_row, place.astype(F32)]
    fields += [cals[p : p + 1] for p in range(6)]
    fields += [ccd[...].reshape(1, obs).astype(F32)]

    basis = spline_basis(frac_row)
    spill = []
    for j in range(3):
        value = jnp.zeros_like(frac_row)
        for a in range(j + 1, 4):
            value = jnp.where(place == SEG + j - a, basis[a], value)
        spill.append(value)
    left = [geom_rows[c] for c, _ in ATT_PAIRS] + [resid_row] * 4
    right = [geom_rows[e] for _, e in ATT_PAIRS] + geom_rows
    zero = jnp.zeros((1, obs), F32)
    both = [
        jnp.concatenate(left[at : at + 8] + [zero] * max(0, at + 8 - 14), 0)
        * jnp.concatenate(right[at : at + 8] + [zero] * max(0, at + 8 - 14), 0)
        for at in (0, 8)
    ]
    sub = lax.broadcasted_iota(jnp.int32, (8, obs), 0)
    for s, (j, d) in enumerate(SPILL):
        pair = spill[j] * spill[j + d]
        other = spill[j] if d == 0 else zero
        terms = [both[0] * pair, both[1] * jnp.where(sub < 2, pair, other)]
        top, rest = split(jnp.concatenate(terms, 0))
        spill_s[16 * s : 16 * s + 16, :] = top
        spill_s[LANES + 16 * s : LANES + 16 * s + 16, :] = rest
    for at in (16 * HIGH, LANES + 16 * HIGH):
        spill_s[at : at + LANES - 16 * HIGH, :] = jnp.zeros((LANES - 16 * HIGH, obs), BF16)

    fields = jnp.concatenate(fields, 0)
    rounded = fields.astype(BF16).astype(F32)
    low_is = sub == low
    for i, part in enumerate((rounded, fields - rounded)):
        for f in range(0, FIELDS, 2):
            pair = [jnp.where(low_is, part[f + n : f + n + 1], 0.0) for n in range(2)]
            at = i * LANES + LOW * f
            val_s[at : at + 16, :] = jnp.concatenate(pair, 0).astype(BF16)
        val_s[i * LANES + SPILL_LANE : (i + 1) * LANES, :] = jnp.zeros((16, obs), BF16)
    code = (high >> 1) * (2 * segs) + 2 * seg + (high & 1)
    for j in range(0, HIGH * segs, 64):
        hot_s[j : j + 64, :] = label_hot(64, 0, (code - j).astype(F32))
    main = nt_dot(hot_s[...], val_s[...])
    main = main[:, :LANES] + main[:, LANES:]
    row = lax.broadcasted_iota(jnp.int32, (2 * segs, obs), 0) >> 1
    sums = nt_dot(jnp.where(row == seg + 1, 1.0, 0.0).astype(BF16), spill_s[...])
    sums = sums[:, :LANES] + sums[:, LANES:]
    lane = lax.broadcasted_iota(jnp.int32, (2 * segs, LANES), 1)
    even = lax.broadcasted_iota(jnp.int32, (2 * segs, LANES), 0) & 1 == 0
    for m in range(HIGH // 2):
        edge = jnp.where(
            even,
            pltpu.roll(sums, SPILL_LANE - 32 * m, 1),
            pltpu.roll(sums, SPILL_LANE - 32 * m - 16, 1),
        )
        tile_s[m] = jnp.where(lane < SPILL_LANE, main[2 * segs * m : 2 * segs * (m + 1)], edge)
        for t in range(segs):
            out[t, :, m * LANES : (m + 1) * LANES] = tile_s[m, 2 * t : 2 * t + 2, :]


def source_kernel(partials, resid, weight, ids, normal, rhs, left_s):
    obs = ids.shape[0]
    wgt, res, idv = (x[...].reshape(1, obs) for x in (weight, resid, ids))
    count = partials.shape[0]
    part = partials[...]
    rows = [part[p : p + 1] for p in range(count)]
    scaled = part * wgt
    scaled_rows = [scaled[p : p + 1] for p in range(count)]
    terms = [scaled_rows[p] * rows[q] for p, q in SRC_PAIRS]
    terms += [scaled_rows[p] * res for p in range(count)]
    terms += [jnp.zeros((32 - len(terms), obs), F32)]
    high, low = split(jnp.concatenate(terms, 0))
    left_s[0:32, :] = high
    left_s[32:64, :] = low
    left = left_s[...]
    step = 256
    for j in range(0, SRC_DEV, step):
        sums = nt_dot(left, onehot(step, j, idv))
        sums = sums[:32] + sums[32:]
        for t, (p, q) in enumerate(SRC_PAIRS):
            normal[p, q : q + 1, j : j + step] = sums[t : t + 1]
            if p != q:
                normal[q, p : p + 1, j : j + step] = sums[t : t + 1]
        rhs[:, j : j + step] = sums[len(SRC_PAIRS) : len(SRC_PAIRS) + count]


def spline_basis(frac):
    remain = 1.0 - frac
    square = frac * frac
    cubic = square * frac
    return [
        remain * remain * remain * (1.0 / 6.0),
        (3.0 * cubic - 6.0 * square + 4.0) * (1.0 / 6.0),
        (-3.0 * cubic + 3.0 * square + 3.0 * frac + 1.0) * (1.0 / 6.0),
        cubic * (1.0 / 6.0),
    ]


def att_terms(rows):
    geoms, frac, resid = rows[:4], rows[4], rows[5]
    basis = spline_basis(frac)
    pairs = [geoms[c] * geoms[e] for c, e in ATT_PAIRS]
    weighted = [geoms[c] * resid for c in range(4)]
    terms = []
    for a in range(4):
        place = GROUP_START[a]
        for c in range(4):
            terms.append((place + c, basis[a] * weighted[c]))
        place = place + 4
        for d in range(4 - a):
            both = basis[a] * basis[a + d]
            for q in range(10):
                terms.append((place + q, both * pairs[q]))
            place = place + 10
        for t in range(place, GROUP_START[a] + GROUP_ROWS[a]):
            terms.append((t, jnp.zeros_like(frac)))
    return terms


def time_kernel(got, out, tile_s, turned_s, att_f, cal_f, att_l, cal_l, knot_hot, ccd_hot, edge_s):
    segs = got.shape[0]
    columns = []
    parity = lax.broadcasted_iota(jnp.int32, (16, LANES), 1) & 1
    for c in range(HIGH // 2):
        for t in range(segs):
            tile_s[c, 2 * t : 2 * t + 2, :] = got[t, :, c * LANES : (c + 1) * LANES]
        turned_s[c] = tile_s[c].T
        edge = turned_s[c, SPILL_LANE:, :]
        for r in range(2):
            columns.append(jnp.sum(jnp.where(parity == r, edge, 0.0), 1, keepdims=True))
        rows = [turned_s[c, LOW * f : LOW * f + LOW, :] for f in range(FIELDS)]
        for t, value in att_terms(rows):
            att_f[c, pl.ds(t, LOW, stride=TERMS_STEP), :] = value
        cals = rows[7:13]
        terms = [cals[p] * cals[q] for p, q in CAL_PAIRS]
        terms += [cals[p] * rows[5] for p in range(6)]
        terms += [jnp.zeros((LOW, LANES), F32)] * (32 - len(terms))
        for t, value in enumerate(terms):
            cal_f[c, pl.ds(t, LOW, stride=CAL_STEP), :] = value
        for l in range(LOW):
            cols = slice(l * LANES, (l + 1) * LANES)
            att_l[c, 0:TERMS, cols], att_l[c, TERMS:, cols] = split(
                att_f[c, l * TERMS_STEP : l * TERMS_STEP + TERMS, :]
            )
            cal_l[c, 0:32, cols], cal_l[c, 32:, cols] = split(
                cal_f[c, l * CAL_STEP : l * CAL_STEP + 32, :]
            )
            for hot, f in ((knot_hot, 6), (ccd_hot, 13)):
                at = LOW * f + l
                hot[c, :, cols] = label_hot(SEG, 0, turned_s[c, at : at + 1, :])
        sums = (nt_dot(att_l[c], knot_hot[c]), nt_dot(cal_l[c], ccd_hot[c]))
        totals = sums if c == 0 else tuple(x + y for x, y in zip(totals, sums))
    main, cal = totals
    main = main[:TERMS] + main[TERMS:]
    cal = cal[:32] + cal[32:]
    lane = lax.broadcasted_iota(jnp.int32, (16, LANES), 1)
    edge_s[...] = jnp.zeros(edge_s.shape, F32)
    for d in range(3):
        block = jnp.zeros((16, LANES), F32)
        for s, (j, gap) in enumerate(SPILL):
            if gap == d:
                block = jnp.where(lane == j, columns[s], block)
        edge_s[4 + 10 * d : 14 + 10 * d, :] = block[0:10]
        if d == 0:
            edge_s[0:4, :] = block[10:14]
    total = main[: GROUP_ROWS[0]]
    for a in range(1, 4):
        n = GROUP_ROWS[a]
        group = pltpu.roll(main[GROUP_START[a] : GROUP_START[a] + n], a, 1)
        group = jnp.where(lax.broadcasted_iota(jnp.int32, (n, SEG), 1) < a, 0.0, group)
        if n < GROUP_ROWS[0]:
            group = jnp.concatenate([group, jnp.zeros((GROUP_ROWS[0] - n, SEG), F32)], 0)
        total = total + group
    for z in range(out.shape[0]):
        out[z, 0:48, 0:LANES] = total[:, :LANES] + edge_s[...]
        out[z, 0:48, LANES:] = total[:, LANES:]
        out[z, 48:72, :] = cal[0:24]
        out[z, 44:47, :] = cal[24:27]


def middle_kernel(parts, out):
    total = parts[0]
    for z in range(1, parts.shape[0]):
        total = total + parts[z]
    for z in range(out.shape[0]):
        out[z] = total


def final_kernel(parts, att_normal, att_rhs, cal_normal, cal_rhs, sum_s):
    total = parts[0]
    for z in range(1, parts.shape[0]):
        total = total + parts[z]
    sum_s[...] = total
    att_rhs[...] = sum_s[0:4, :]
    for d in range(4):
        for q, (c, e) in enumerate(ATT_PAIRS):
            row = sum_s[4 + 10 * d + q : 5 + 10 * d + q, :]
            att_normal[d, c, e : e + 1, :] = row
            if c != e:
                att_normal[d, e, c : c + 1, :] = row

    def cal_row(t):
        at = 48 + t if t < 24 else 20 + t
        return sum_s[at : at + 1, :]

    for t, (p, q) in enumerate(CAL_PAIRS):
        cal_normal[p, q : q + 1, :] = cal_row(t)
        if p != q:
            cal_normal[q, p : p + 1, :] = cal_row(t)
    for p in range(6):
        cal_rhs[p : p + 1, :] = cal_row(21 + p)


def exchange(blocks, groups):
    return lax.all_to_all(
        blocks, "src", split_axis=0, concat_axis=0, tiled=True, axis_index_groups=groups
    )


def call(kernel, out_shape, scratch, vmem_mib, cost, *args, space=pltpu.VMEM):
    return pl.pallas_call(
        kernel,
        out_shape=out_shape,
        in_specs=[pl.BlockSpec(memory_space=space)] * len(args),
        scratch_shapes=scratch,
        compiler_params=pltpu.CompilerParams(vmem_limit_bytes=vmem_mib * 1024 * 1024),
        cost_estimate=pl.CostEstimate(flops=cost, bytes_accessed=200000, transcendentals=0),
    )(*args)


def shape(*dims):
    return jax.ShapeDtypeStruct(dims, F32)


def local(
    src_partials,
    att_geom,
    spline_frac,
    cal_partials,
    residual,
    weight,
    source_ids,
    knot_ids,
    ccd_ids,
):
    obs = residual.shape[0]
    tm_count = lax.axis_size("tm")
    z_count = lax.axis_size("src")
    rows = (att_geom, spline_frac, cal_partials, residual, weight, knot_ids, ccd_ids)
    send = call(
        pack_kernel,
        shape(tm_count, 2, HIGH // 2 * LANES),
        [
            pltpu.VMEM((HIGH * tm_count, obs), BF16),
            pltpu.VMEM((2 * LANES, obs), BF16),
            pltpu.VMEM((2 * LANES, obs), BF16),
            pltpu.VMEM((HIGH // 2, 2 * tm_count, LANES), F32),
        ]
        + [pltpu.VMEM(x.shape, x.dtype) for x in rows]
        + [pltpu.SemaphoreType.DMA((len(rows),))],
        PACK_MIB,
        1000000000,
        *rows,
        space=pltpu.HBM,
    )
    got = lax.all_to_all(send, "tm", split_axis=0, concat_axis=0, tiled=True)
    src_normal, src_rhs = call(
        source_kernel,
        (shape(5, 5, SRC_DEV), shape(5, SRC_DEV)),
        [pltpu.VMEM((64, obs), BF16)],
        12,
        4000000000,
        src_partials,
        residual,
        weight,
        source_ids,
    )
    got, src_normal, src_rhs = lax.optimization_barrier((got, src_normal, src_rhs))
    chunks = HIGH // 2
    depth = LOW * LANES
    sums = call(
        time_kernel,
        shape(2, 72, SEG),
        [
            pltpu.VMEM((chunks, 2 * tm_count, LANES), F32),
            pltpu.VMEM((chunks, LANES, LANES), F32),
            pltpu.VMEM((chunks, LOW * TERMS_STEP, LANES), F32),
            pltpu.VMEM((chunks, LOW * CAL_STEP, LANES), F32),
            pltpu.VMEM((chunks, 2 * TERMS, depth), BF16),
            pltpu.VMEM((chunks, 64, depth), BF16),
            pltpu.VMEM((chunks, SEG, depth), BF16),
            pltpu.VMEM((chunks, SEG, depth), BF16),
            pltpu.VMEM((48, LANES), F32),
        ],
        24,
        1000000000,
        got,
    )
    pairs = [[2 * g, 2 * g + 1] for g in range(z_count // 2)]
    ranks = [[2 * g + i for g in range(z_count // 2)] for i in range(2)]
    parts = exchange(sums, pairs)
    parts = call(middle_kernel, shape(z_count // 2, 72, SEG), [], 8, 1000000, parts)
    parts = exchange(parts, ranks)
    att_normal, att_rhs, cal_normal, cal_rhs = call(
        final_kernel,
        (shape(4, 4, 4, SEG), shape(4, SEG), shape(6, 6, SEG), shape(6, SEG)),
        [pltpu.VMEM((72, SEG), F32)],
        8,
        1000000,
        parts,
    )
    return (src_normal, src_rhs, att_normal, att_rhs, cal_normal, cal_rhs)


def solution(mesh):
    both = ("tm", "src")
    in_specs = (
        P(None, both),
        P(None, both),
        P(both),
        P(None, both),
        P(both),
        P(both),
        P(both),
        P(both),
        P(both),
    )
    out_specs = (
        P(None, None, both),
        P(None, both),
        P(None, None, None, "tm"),
        P(None, "tm"),
        P(None, None, "tm"),
        P(None, "tm"),
    )
    return jax.shard_map(local, mesh=mesh, in_specs=in_specs, out_specs=out_specs, check_vma=False)
```

```python
import jax
import jax.numpy as jnp
from jax import lax
from jax.experimental import pallas as pl
from jax.experimental.pallas import tpu as pltpu
from jax.sharding import PartitionSpec as P

SRC_DEV = 1024
SEG = 256
LANES = 128
F32 = jnp.float32
BF16 = jnp.bfloat16

LOW = 8
HIGH = 6
FIELDS = 14
SPILL = [(0, 0), (1, 0), (2, 0), (0, 1), (1, 1), (0, 2)]
SPILL_LANE = LOW * FIELDS
ATT_PAIRS = [(c, e) for c in range(4) for e in range(c, 4)]
CAL_PAIRS = [(p, q) for p in range(6) for q in range(p, 6)]
SRC_PAIRS = [(p, q) for p in range(5) for q in range(p, 5)]
GROUP_ROWS = [48, 40, 24, 16]
GROUP_START = [0, 48, 88, 112]
TERMS = 128
PACK_MIB = 56
TERMS_STEP, CAL_STEP = TERMS + 1, 32 + 1


def nt_dot(left, right):
    return lax.dot_general(
        left, right, (((1,), (1,)), ((), ())), preferred_element_type=F32
    )


def split(x):
    high = x.astype(BF16)
    return high, (x - high.astype(F32)).astype(BF16)


def onehot(rows, first, ids):
    place = lax.broadcasted_iota(jnp.int32, (rows, ids.shape[1]), 0) + first
    return jnp.where(place == ids, 1.0, 0.0).astype(BF16)


def label_hot(rows, first, ids):
    place = (lax.broadcasted_iota(jnp.int32, (rows, ids.shape[1]), 0) + first).astype(F32).astype(BF16)
    same = place == jnp.broadcast_to(ids, place.shape).astype(BF16)
    return jnp.where(same, jnp.ones_like(place), jnp.zeros_like(place))


def pack_kernel(*refs):
    count = 7
    out = refs[count]
    hot_s, val_s, spill_s, tile_s = refs[count + 1 : count + 5]
    held = refs[count + 5 : -1]
    copies = [
        pltpu.make_async_copy(refs[i], held[i], refs[-1].at[i]) for i in range(count)
    ]
    for i in (5, 0, 1, 2, 3, 4, 6):
        copies[i].start()
    geom, frac, cal, resid, weight, knot, ccd = held
    copies[5].wait()
    obs = knot.shape[0]
    segs = out.shape[0]
    chunk = 256
    blocks = obs // chunk
    knots = knot[...].reshape(1, obs)
    seg = knots // SEG
    member = label_hot(segs, 0, seg.astype(F32))
    before = lax.broadcasted_iota(jnp.int32, (chunk, chunk), 0) < lax.broadcasted_iota(
        jnp.int32, (chunk, chunk), 1
    )
    before = jnp.where(before, 1.0, 0.0).astype(BF16)
    counter = jnp.concatenate([before, jnp.ones((chunk, LANES), BF16)], 1)
    carry = jnp.zeros((segs, LANES), F32)
    ranks = []
    for b in range(blocks):
        here = member[:, b * chunk : (b + 1) * chunk]
        counts = jnp.dot(here, counter, preferred_element_type=F32)
        for half in range(chunk // LANES):
            cols = slice(half * LANES, (half + 1) * LANES)
            ranks.append(
                jnp.sum(here[:, cols].astype(F32) * (counts[:, cols] + carry), 0, keepdims=True)
            )
        carry = carry + counts[:, chunk:]
    rank = jnp.concatenate(ranks, 1).astype(jnp.int32)
    high = rank >> 3
    low = rank & 7

    for i in (0, 1, 2, 3, 4, 6):
        copies[i].wait()
    scale = jnp.sqrt(weight[...].reshape(1, obs))
    geoms = geom[...] * scale
    cals = cal[...] * scale
    place = knots - SEG * seg
    frac_row = frac[...].reshape(1, obs)
    geom_rows = [geoms[c : c + 1] for c in range(4)]
    resid_row = resid[...].reshape(1, obs) * scale
    fields = geom_rows + [frac_row, resid_row, place.astype(F32)]
    fields += [cals[p : p + 1] for p in range(6)]
    fields += [ccd[...].reshape(1, obs).astype(F32)]

    basis = spline_basis(frac_row)
    spill = []
    for j in range(3):
        value = jnp.zeros_like(frac_row)
        for a in range(j + 1, 4):
            value = jnp.where(place == SEG + j - a, basis[a], value)
        spill.append(value)
    left = [geom_rows[c] for c, _ in ATT_PAIRS] + [resid_row] * 4
    right = [geom_rows[e] for _, e in ATT_PAIRS] + geom_rows
    zero = jnp.zeros((1, obs), F32)
    both = [
        jnp.concatenate(left[at : at + 8] + [zero] * max(0, at + 8 - 14), 0)
        * jnp.concatenate(right[at : at + 8] + [zero] * max(0, at + 8 - 14), 0)
        for at in (0, 8)
    ]
    sub = lax.broadcasted_iota(jnp.int32, (8, obs), 0)
    for s, (j, d) in enumerate(SPILL):
        pair = spill[j] * spill[j + d]
        other = spill[j] if d == 0 else zero
        terms = [both[0] * pair, both[1] * jnp.where(sub < 2, pair, other)]
        top, rest = split(jnp.concatenate(terms, 0))
        spill_s[16 * s : 16 * s + 16, :] = top
        spill_s[LANES + 16 * s : LANES + 16 * s + 16, :] = rest
    for at in (16 * HIGH, LANES + 16 * HIGH):
        spill_s[at : at + LANES - 16 * HIGH, :] = jnp.zeros((LANES - 16 * HIGH, obs), BF16)

    fields = jnp.concatenate(fields, 0)
    rounded = fields.astype(BF16).astype(F32)
    low_is = sub == low
    for i, part in enumerate((rounded, fields - rounded)):
        for f in range(0, FIELDS, 2):
            pair = [jnp.where(low_is, part[f + n : f + n + 1], 0.0) for n in range(2)]
            at = i * LANES + LOW * f
            val_s[at : at + 16, :] = jnp.concatenate(pair, 0).astype(BF16)
        val_s[i * LANES + SPILL_LANE : (i + 1) * LANES, :] = jnp.zeros((16, obs), BF16)
    code = (high >> 1) * (2 * segs) + 2 * seg + (high & 1)
    for j in range(0, HIGH * segs, 64):
        hot_s[j : j + 64, :] = label_hot(64, 0, (code - j).astype(F32))
    main = nt_dot(hot_s[...], val_s[...])
    main = main[:, :LANES] + main[:, LANES:]
    row = lax.broadcasted_iota(jnp.int32, (2 * segs, obs), 0) >> 1
    sums = nt_dot(jnp.where(row == seg + 1, 1.0, 0.0).astype(BF16), spill_s[...])
    sums = sums[:, :LANES] + sums[:, LANES:]
    lane = lax.broadcasted_iota(jnp.int32, (2 * segs, LANES), 1)
    even = lax.broadcasted_iota(jnp.int32, (2 * segs, LANES), 0) & 1 == 0
    for m in range(HIGH // 2):
        edge = jnp.where(
            even,
            pltpu.roll(sums, SPILL_LANE - 32 * m, 1),
            pltpu.roll(sums, SPILL_LANE - 32 * m - 16, 1),
        )
        tile_s[m] = jnp.where(lane < SPILL_LANE, main[2 * segs * m : 2 * segs * (m + 1)], edge)
        for t in range(segs):
            out[t, :, m * LANES : (m + 1) * LANES] = tile_s[m, 2 * t : 2 * t + 2, :]


def source_kernel(partials, resid, weight, ids, normal, rhs, left_s):
    obs = ids.shape[0]
    wgt, res, idv = (x[...].reshape(1, obs) for x in (weight, resid, ids))
    count = partials.shape[0]
    part = partials[...]
    rows = [part[p : p + 1] for p in range(count)]
    scaled = part * wgt
    scaled_rows = [scaled[p : p + 1] for p in range(count)]
    terms = [scaled_rows[p] * rows[q] for p, q in SRC_PAIRS]
    terms += [scaled_rows[p] * res for p in range(count)]
    terms += [jnp.zeros((32 - len(terms), obs), F32)]
    high, low = split(jnp.concatenate(terms, 0))
    left_s[0:32, :] = high
    left_s[32:64, :] = low
    left = left_s[...]
    step = 256
    for j in range(0, SRC_DEV, step):
        sums = nt_dot(left, onehot(step, j, idv))
        sums = sums[:32] + sums[32:]
        for t, (p, q) in enumerate(SRC_PAIRS):
            normal[p, q : q + 1, j : j + step] = sums[t : t + 1]
            if p != q:
                normal[q, p : p + 1, j : j + step] = sums[t : t + 1]
        rhs[:, j : j + step] = sums[len(SRC_PAIRS) : len(SRC_PAIRS) + count]


def spline_basis(frac):
    remain = 1.0 - frac
    square = frac * frac
    cubic = square * frac
    return [
        remain * remain * remain * (1.0 / 6.0),
        (3.0 * cubic - 6.0 * square + 4.0) * (1.0 / 6.0),
        (-3.0 * cubic + 3.0 * square + 3.0 * frac + 1.0) * (1.0 / 6.0),
        cubic * (1.0 / 6.0),
    ]


def att_terms(rows):
    geoms, frac, resid = rows[:4], rows[4], rows[5]
    basis = spline_basis(frac)
    pairs = [geoms[c] * geoms[e] for c, e in ATT_PAIRS]
    weighted = [geoms[c] * resid for c in range(4)]
    terms = []
    for a in range(4):
        place = GROUP_START[a]
        for c in range(4):
            terms.append((place + c, basis[a] * weighted[c]))
        place = place + 4
        for d in range(4 - a):
            both = basis[a] * basis[a + d]
            for q in range(10):
                terms.append((place + q, both * pairs[q]))
            place = place + 10
        for t in range(place, GROUP_START[a] + GROUP_ROWS[a]):
            terms.append((t, jnp.zeros_like(frac)))
    return terms


def time_kernel(got, out, tile_s, turned_s, att_f, cal_f, att_l, cal_l, knot_hot, ccd_hot, edge_s):
    segs = got.shape[0]
    columns = []
    parity = lax.broadcasted_iota(jnp.int32, (16, LANES), 1) & 1
    for c in range(HIGH // 2):
        for t in range(segs):
            tile_s[c, 2 * t : 2 * t + 2, :] = got[t, :, c * LANES : (c + 1) * LANES]
        turned_s[c] = tile_s[c].T
        edge = turned_s[c, SPILL_LANE:, :]
        for r in range(2):
            columns.append(jnp.sum(jnp.where(parity == r, edge, 0.0), 1, keepdims=True))
        rows = [turned_s[c, LOW * f : LOW * f + LOW, :] for f in range(FIELDS)]
        for t, value in att_terms(rows):
            att_f[c, pl.ds(t, LOW, stride=TERMS_STEP), :] = value
        cals = rows[7:13]
        terms = [cals[p] * cals[q] for p, q in CAL_PAIRS]
        terms += [cals[p] * rows[5] for p in range(6)]
        terms += [jnp.zeros((LOW, LANES), F32)] * (32 - len(terms))
        for t, value in enumerate(terms):
            cal_f[c, pl.ds(t, LOW, stride=CAL_STEP), :] = value
        for l in range(LOW):
            cols = slice(l * LANES, (l + 1) * LANES)
            att_l[c, 0:TERMS, cols], att_l[c, TERMS:, cols] = split(
                att_f[c, l * TERMS_STEP : l * TERMS_STEP + TERMS, :]
            )
            cal_l[c, 0:32, cols], cal_l[c, 32:, cols] = split(
                cal_f[c, l * CAL_STEP : l * CAL_STEP + 32, :]
            )
            for hot, f in ((knot_hot, 6), (ccd_hot, 13)):
                at = LOW * f + l
                hot[c, :, cols] = label_hot(SEG, 0, turned_s[c, at : at + 1, :])
        sums = (nt_dot(att_l[c], knot_hot[c]), nt_dot(cal_l[c], ccd_hot[c]))
        totals = sums if c == 0 else tuple(x + y for x, y in zip(totals, sums))
    main, cal = totals
    main = main[:TERMS] + main[TERMS:]
    cal = cal[:32] + cal[32:]
    lane = lax.broadcasted_iota(jnp.int32, (16, LANES), 1)
    edge_s[...] = jnp.zeros(edge_s.shape, F32)
    for d in range(3):
        block = jnp.zeros((16, LANES), F32)
        for s, (j, gap) in enumerate(SPILL):
            if gap == d:
                block = jnp.where(lane == j, columns[s], block)
        edge_s[4 + 10 * d : 14 + 10 * d, :] = block[0:10]
        if d == 0:
            edge_s[0:4, :] = block[10:14]
    total = main[: GROUP_ROWS[0]]
    for a in range(1, 4):
        n = GROUP_ROWS[a]
        group = pltpu.roll(main[GROUP_START[a] : GROUP_START[a] + n], a, 1)
        group = jnp.where(lax.broadcasted_iota(jnp.int32, (n, SEG), 1) < a, 0.0, group)
        if n < GROUP_ROWS[0]:
            group = jnp.concatenate([group, jnp.zeros((GROUP_ROWS[0] - n, SEG), F32)], 0)
        total = total + group
    for z in range(out.shape[0]):
        out[z, 0:48, 0:LANES] = total[:, :LANES] + edge_s[...]
        out[z, 0:48, LANES:] = total[:, LANES:]
        out[z, 48:72, :] = cal[0:24]
        out[z, 44:47, :] = cal[24:27]


def middle_kernel(parts, out):
    total = parts[0]
    for z in range(1, parts.shape[0]):
        total = total + parts[z]
    for z in range(out.shape[0]):
        out[z] = total


def final_kernel(parts, att_normal, att_rhs, cal_normal, cal_rhs, sum_s):
    total = parts[0]
    for z in range(1, parts.shape[0]):
        total = total + parts[z]
    sum_s[...] = total
    att_rhs[...] = sum_s[0:4, :]
    for d in range(4):
        for q, (c, e) in enumerate(ATT_PAIRS):
            row = sum_s[4 + 10 * d + q : 5 + 10 * d + q, :]
            att_normal[d, c, e : e + 1, :] = row
            if c != e:
                att_normal[d, e, c : c + 1, :] = row

    def cal_row(t):
        at = 48 + t if t < 24 else 20 + t
        return sum_s[at : at + 1, :]

    for t, (p, q) in enumerate(CAL_PAIRS):
        cal_normal[p, q : q + 1, :] = cal_row(t)
        if p != q:
            cal_normal[q, p : p + 1, :] = cal_row(t)
    for p in range(6):
        cal_rhs[p : p + 1, :] = cal_row(21 + p)


def exchange(blocks, groups):
    return lax.all_to_all(
        blocks, "src", split_axis=0, concat_axis=0, tiled=True, axis_index_groups=groups
    )


def call(kernel, out_shape, scratch, vmem_mib, cost, *args, space=pltpu.VMEM):
    return pl.pallas_call(
        kernel,
        out_shape=out_shape,
        in_specs=[pl.BlockSpec(memory_space=space)] * len(args),
        scratch_shapes=scratch,
        compiler_params=pltpu.CompilerParams(vmem_limit_bytes=vmem_mib * 1024 * 1024),
        cost_estimate=pl.CostEstimate(flops=cost, bytes_accessed=200000, transcendentals=0),
    )(*args)


def shape(*dims):
    return jax.ShapeDtypeStruct(dims, F32)


def local(
    src_partials,
    att_geom,
    spline_frac,
    cal_partials,
    residual,
    weight,
    source_ids,
    knot_ids,
    ccd_ids,
):
    obs = residual.shape[0]
    tm_count = lax.axis_size("tm")
    z_count = lax.axis_size("src")
    rows = (att_geom, spline_frac, cal_partials, residual, weight, knot_ids, ccd_ids)
    send = call(
        pack_kernel,
        shape(tm_count, 2, HIGH // 2 * LANES),
        [
            pltpu.VMEM((HIGH * tm_count, obs), BF16),
            pltpu.VMEM((2 * LANES, obs), BF16),
            pltpu.VMEM((2 * LANES, obs), BF16),
            pltpu.VMEM((HIGH // 2, 2 * tm_count, LANES), F32),
        ]
        + [pltpu.VMEM(x.shape, x.dtype) for x in rows]
        + [pltpu.SemaphoreType.DMA((len(rows),))],
        PACK_MIB,
        1000000000,
        *rows,
        space=pltpu.HBM,
    )
    got = lax.all_to_all(send, "tm", split_axis=0, concat_axis=0, tiled=True)
    src_normal, src_rhs = call(
        source_kernel,
        (shape(5, 5, SRC_DEV), shape(5, SRC_DEV)),
        [pltpu.VMEM((64, obs), BF16)],
        12,
        4000000000,
        src_partials,
        residual,
        weight,
        source_ids,
    )
    got, src_normal, src_rhs = lax.optimization_barrier((got, src_normal, src_rhs))
    chunks = HIGH // 2
    depth = LOW * LANES
    sums = call(
        time_kernel,
        shape(2, 72, SEG),
        [
            pltpu.VMEM((chunks, 2 * tm_count, LANES), F32),
            pltpu.VMEM((chunks, LANES, LANES), F32),
            pltpu.VMEM((chunks, LOW * TERMS_STEP, LANES), F32),
            pltpu.VMEM((chunks, LOW * CAL_STEP, LANES), F32),
            pltpu.VMEM((chunks, 2 * TERMS, depth), BF16),
            pltpu.VMEM((chunks, 64, depth), BF16),
            pltpu.VMEM((chunks, SEG, depth), BF16),
            pltpu.VMEM((chunks, SEG, depth), BF16),
            pltpu.VMEM((48, LANES), F32),
        ],
        24,
        1000000000,
        got,
    )
    pairs = [[2 * g, 2 * g + 1] for g in range(z_count // 2)]
    ranks = [[2 * g + i for g in reversed(range(z_count // 2))] for i in range(2)]
    parts = exchange(sums, pairs)
    parts = call(middle_kernel, shape(z_count // 2, 72, SEG), [], 8, 1000000, parts)
    parts = exchange(parts, ranks)
    att_normal, att_rhs, cal_normal, cal_rhs = call(
        final_kernel,
        (shape(4, 4, 4, SEG), shape(4, SEG), shape(6, 6, SEG), shape(6, SEG)),
        [pltpu.VMEM((72, SEG), F32)],
        8,
        1000000,
        parts,
    )
    return (src_normal, src_rhs, att_normal, att_rhs, cal_normal, cal_rhs)


def solution(mesh):
    both = ("tm", "src")
    in_specs = (
        P(None, both),
        P(None, both),
        P(both),
        P(None, both),
        P(both),
        P(both),
        P(both),
        P(both),
        P(both),
    )
    out_specs = (
        P(None, None, both),
        P(None, both),
        P(None, None, None, "tm"),
        P(None, "tm"),
        P(None, None, "tm"),
        P(None, "tm"),
    )
    return jax.shard_map(local, mesh=mesh, in_specs=in_specs, out_specs=out_specs, check_vma=False)
```

```python
import jax
import jax.numpy as jnp
from jax import lax
from jax.experimental import pallas as pl
from jax.experimental.pallas import tpu as pltpu
from jax.sharding import PartitionSpec as P

SRC_DEV = 1024
SEG = 256
LANES = 128
F32 = jnp.float32
BF16 = jnp.bfloat16

LOW = 8
HIGH = 6
FIELDS = 14
SPILL = [(0, 0), (1, 0), (2, 0), (0, 1), (1, 1), (0, 2)]
SPILL_LANE = LOW * FIELDS
ATT_PAIRS = [(c, e) for c in range(4) for e in range(c, 4)]
CAL_PAIRS = [(p, q) for p in range(6) for q in range(p, 6)]
SRC_PAIRS = [(p, q) for p in range(5) for q in range(p, 5)]
GROUP_ROWS = [48, 40, 24, 16]
GROUP_START = [0, 48, 88, 112]
TERMS = 128
PACK_MIB = 56
TERMS_STEP, CAL_STEP = TERMS + 1, 32 + 1


def nt_dot(left, right):
    return lax.dot_general(
        left, right, (((1,), (1,)), ((), ())), preferred_element_type=F32
    )


def split(x):
    high = x.astype(BF16)
    return high, (x - high.astype(F32)).astype(BF16)


def onehot(rows, first, ids):
    place = lax.broadcasted_iota(jnp.int32, (rows, ids.shape[1]), 0) + first
    return jnp.where(place == ids, 1.0, 0.0).astype(BF16)


def label_hot(rows, first, ids):
    place = (lax.broadcasted_iota(jnp.int32, (rows, ids.shape[1]), 0) + first).astype(F32).astype(BF16)
    same = place == jnp.broadcast_to(ids, place.shape).astype(BF16)
    return jnp.where(same, jnp.ones_like(place), jnp.zeros_like(place))


def pack_kernel(*refs):
    count = 7
    out = refs[count]
    hot_s, val_s, spill_s, tile_s = refs[count + 1 : count + 5]
    held = refs[count + 5 : -1]
    copies = [
        pltpu.make_async_copy(refs[i], held[i], refs[-1].at[i]) for i in range(count)
    ]
    for i in (5, 0, 1, 2, 3, 4, 6):
        copies[i].start()
    geom, frac, cal, resid, weight, knot, ccd = held
    copies[5].wait()
    obs = knot.shape[0]
    segs = out.shape[0]
    chunk = 256
    blocks = obs // chunk
    knots = knot[...].reshape(1, obs)
    seg = knots // SEG
    member = label_hot(segs, 0, seg.astype(F32))
    before = lax.broadcasted_iota(jnp.int32, (chunk, chunk), 0) < lax.broadcasted_iota(
        jnp.int32, (chunk, chunk), 1
    )
    before = jnp.where(before, 1.0, 0.0).astype(BF16)
    counter = jnp.concatenate([before, jnp.ones((chunk, LANES), BF16)], 1)
    carry = jnp.zeros((segs, LANES), F32)
    ranks = []
    for b in range(blocks):
        here = member[:, b * chunk : (b + 1) * chunk]
        counts = jnp.dot(here, counter, preferred_element_type=F32)
        for half in range(chunk // LANES):
            cols = slice(half * LANES, (half + 1) * LANES)
            ranks.append(
                jnp.sum(here[:, cols].astype(F32) * (counts[:, cols] + carry), 0, keepdims=True)
            )
        carry = carry + counts[:, chunk:]
    rank = jnp.concatenate(ranks, 1).astype(jnp.int32)
    high = rank >> 3
    low = rank & 7

    for i in (0, 1, 2, 3, 4, 6):
        copies[i].wait()
    scale = jnp.sqrt(weight[...].reshape(1, obs))
    geoms = geom[...] * scale
    cals = cal[...] * scale
    place = knots - SEG * seg
    frac_row = frac[...].reshape(1, obs)
    geom_rows = [geoms[c : c + 1] for c in range(4)]
    resid_row = resid[...].reshape(1, obs) * scale
    fields = geom_rows + [frac_row, resid_row, place.astype(F32)]
    fields += [cals[p : p + 1] for p in range(6)]
    fields += [ccd[...].reshape(1, obs).astype(F32)]

    basis = spline_basis(frac_row)
    spill = []
    for j in range(3):
        value = jnp.zeros_like(frac_row)
        for a in range(j + 1, 4):
            value = jnp.where(place == SEG + j - a, basis[a], value)
        spill.append(value)
    left = [geom_rows[c] for c, _ in ATT_PAIRS] + [resid_row] * 4
    right = [geom_rows[e] for _, e in ATT_PAIRS] + geom_rows
    zero = jnp.zeros((1, obs), F32)
    both = [
        jnp.concatenate(left[at : at + 8] + [zero] * max(0, at + 8 - 14), 0)
        * jnp.concatenate(right[at : at + 8] + [zero] * max(0, at + 8 - 14), 0)
        for at in (0, 8)
    ]
    sub = lax.broadcasted_iota(jnp.int32, (8, obs), 0)
    for s, (j, d) in enumerate(SPILL):
        pair = spill[j] * spill[j + d]
        other = spill[j] if d == 0 else zero
        terms = [both[0] * pair, both[1] * jnp.where(sub < 2, pair, other)]
        top, rest = split(jnp.concatenate(terms, 0))
        spill_s[16 * s : 16 * s + 16, :] = top
        spill_s[LANES + 16 * s : LANES + 16 * s + 16, :] = rest
    for at in (16 * HIGH, LANES + 16 * HIGH):
        spill_s[at : at + LANES - 16 * HIGH, :] = jnp.zeros((LANES - 16 * HIGH, obs), BF16)

    fields = jnp.concatenate(fields, 0)
    rounded = fields.astype(BF16).astype(F32)
    low_is = sub == low
    for i, part in enumerate((rounded, fields - rounded)):
        for f in range(0, FIELDS, 2):
            pair = [jnp.where(low_is, part[f + n : f + n + 1], 0.0) for n in range(2)]
            at = i * LANES + LOW * f
            val_s[at : at + 16, :] = jnp.concatenate(pair, 0).astype(BF16)
        val_s[i * LANES + SPILL_LANE : (i + 1) * LANES, :] = jnp.zeros((16, obs), BF16)
    code = (high >> 1) * (2 * segs) + 2 * seg + (high & 1)
    for j in range(0, HIGH * segs, 64):
        hot_s[j : j + 64, :] = label_hot(64, 0, (code - j).astype(F32))
    main = nt_dot(hot_s[...], val_s[...])
    main = main[:, :LANES] + main[:, LANES:]
    row = lax.broadcasted_iota(jnp.int32, (2 * segs, obs), 0) >> 1
    sums = nt_dot(jnp.where(row == seg + 1, 1.0, 0.0).astype(BF16), spill_s[...])
    sums = sums[:, :LANES] + sums[:, LANES:]
    lane = lax.broadcasted_iota(jnp.int32, (2 * segs, LANES), 1)
    even = lax.broadcasted_iota(jnp.int32, (2 * segs, LANES), 0) & 1 == 0
    for m in range(HIGH // 2):
        edge = jnp.where(
            even,
            pltpu.roll(sums, SPILL_LANE - 32 * m, 1),
            pltpu.roll(sums, SPILL_LANE - 32 * m - 16, 1),
        )
        tile_s[m] = jnp.where(lane < SPILL_LANE, main[2 * segs * m : 2 * segs * (m + 1)], edge)
        for t in range(segs):
            out[t, :, m * LANES : (m + 1) * LANES] = tile_s[m, 2 * t : 2 * t + 2, :]


def source_kernel(partials, resid, weight, ids, normal, rhs, left_s):
    obs = ids.shape[0]
    wgt, res, idv = (x[...].reshape(1, obs) for x in (weight, resid, ids))
    count = partials.shape[0]
    part = partials[...]
    rows = [part[p : p + 1] for p in range(count)]
    scaled = part * wgt
    scaled_rows = [scaled[p : p + 1] for p in range(count)]
    terms = [scaled_rows[p] * rows[q] for p, q in SRC_PAIRS]
    terms += [scaled_rows[p] * res for p in range(count)]
    terms += [jnp.zeros((32 - len(terms), obs), F32)]
    high, low = split(jnp.concatenate(terms, 0))
    left_s[0:32, :] = high
    left_s[32:64, :] = low
    left = left_s[...]
    step = 256
    for j in range(0, SRC_DEV, step):
        sums = nt_dot(left, onehot(step, j, idv))
        sums = sums[:32] + sums[32:]
        for t, (p, q) in enumerate(SRC_PAIRS):
            normal[p, q : q + 1, j : j + step] = sums[t : t + 1]
            if p != q:
                normal[q, p : p + 1, j : j + step] = sums[t : t + 1]
        rhs[:, j : j + step] = sums[len(SRC_PAIRS) : len(SRC_PAIRS) + count]


def spline_basis(frac):
    remain = 1.0 - frac
    square = frac * frac
    cubic = square * frac
    return [
        remain * remain * remain * (1.0 / 6.0),
        (3.0 * cubic - 6.0 * square + 4.0) * (1.0 / 6.0),
        (-3.0 * cubic + 3.0 * square + 3.0 * frac + 1.0) * (1.0 / 6.0),
        cubic * (1.0 / 6.0),
    ]


def att_terms(rows):
    geoms, frac, resid = rows[:4], rows[4], rows[5]
    basis = spline_basis(frac)
    pairs = [geoms[c] * geoms[e] for c, e in ATT_PAIRS]
    weighted = [geoms[c] * resid for c in range(4)]
    terms = []
    for a in range(4):
        place = GROUP_START[a]
        for c in range(4):
            terms.append((place + c, basis[a] * weighted[c]))
        place = place + 4
        for d in range(4 - a):
            both = basis[a] * basis[a + d]
            for q in range(10):
                terms.append((place + q, both * pairs[q]))
            place = place + 10
        for t in range(place, GROUP_START[a] + GROUP_ROWS[a]):
            terms.append((t, jnp.zeros_like(frac)))
    return terms


def time_kernel(got, out, tile_s, turned_s, att_f, cal_f, att_l, cal_l, knot_hot, ccd_hot, edge_s):
    segs = got.shape[0]
    columns = []
    parity = lax.broadcasted_iota(jnp.int32, (16, LANES), 1) & 1
    for c in range(HIGH // 2):
        for t in range(segs):
            tile_s[c, 2 * t : 2 * t + 2, :] = got[t, :, c * LANES : (c + 1) * LANES]
        turned_s[c] = tile_s[c].T
        edge = turned_s[c, SPILL_LANE:, :]
        for r in range(2):
            columns.append(jnp.sum(jnp.where(parity == r, edge, 0.0), 1, keepdims=True))
        rows = [turned_s[c, LOW * f : LOW * f + LOW, :] for f in range(FIELDS)]
        for t, value in att_terms(rows):
            att_f[c, pl.ds(t, LOW, stride=TERMS_STEP), :] = value
        cals = rows[7:13]
        terms = [cals[p] * cals[q] for p, q in CAL_PAIRS]
        terms += [cals[p] * rows[5] for p in range(6)]
        terms += [jnp.zeros((LOW, LANES), F32)] * (32 - len(terms))
        for t, value in enumerate(terms):
            cal_f[c, pl.ds(t, LOW, stride=CAL_STEP), :] = value
        for l in range(LOW):
            cols = slice(l * LANES, (l + 1) * LANES)
            att_l[c, 0:TERMS, cols], att_l[c, TERMS:, cols] = split(
                att_f[c, l * TERMS_STEP : l * TERMS_STEP + TERMS, :]
            )
            cal_l[c, 0:32, cols], cal_l[c, 32:, cols] = split(
                cal_f[c, l * CAL_STEP : l * CAL_STEP + 32, :]
            )
            for hot, f in ((knot_hot, 6), (ccd_hot, 13)):
                at = LOW * f + l
                hot[c, :, cols] = label_hot(SEG, 0, turned_s[c, at : at + 1, :])
        sums = (nt_dot(att_l[c], knot_hot[c]), nt_dot(cal_l[c], ccd_hot[c]))
        totals = sums if c == 0 else tuple(x + y for x, y in zip(totals, sums))
    main, cal = totals
    main = main[:TERMS] + main[TERMS:]
    cal = cal[:32] + cal[32:]
    lane = lax.broadcasted_iota(jnp.int32, (16, LANES), 1)
    edge_s[...] = jnp.zeros(edge_s.shape, F32)
    for d in range(3):
        block = jnp.zeros((16, LANES), F32)
        for s, (j, gap) in enumerate(SPILL):
            if gap == d:
                block = jnp.where(lane == j, columns[s], block)
        edge_s[4 + 10 * d : 14 + 10 * d, :] = block[0:10]
        if d == 0:
            edge_s[0:4, :] = block[10:14]
    total = main[: GROUP_ROWS[0]]
    for a in range(1, 4):
        n = GROUP_ROWS[a]
        group = pltpu.roll(main[GROUP_START[a] : GROUP_START[a] + n], a, 1)
        group = jnp.where(lax.broadcasted_iota(jnp.int32, (n, SEG), 1) < a, 0.0, group)
        if n < GROUP_ROWS[0]:
            group = jnp.concatenate([group, jnp.zeros((GROUP_ROWS[0] - n, SEG), F32)], 0)
        total = total + group
    for z in range(out.shape[0]):
        out[z, 0:48, 0:LANES] = total[:, :LANES] + edge_s[...]
        out[z, 0:48, LANES:] = total[:, LANES:]
        out[z, 48:72, :] = cal[0:24]
        out[z, 44:47, :] = cal[24:27]


def middle_kernel(parts, out):
    total = parts[0]
    for z in range(1, parts.shape[0]):
        total = total + parts[z]
    for z in range(out.shape[0]):
        out[z] = total


def final_kernel(parts, att_normal, att_rhs, cal_normal, cal_rhs, sum_s):
    total = parts[0]
    for z in range(1, parts.shape[0]):
        total = total + parts[z]
    sum_s[...] = total
    att_rhs[...] = sum_s[0:4, :]
    for d in range(4):
        for q, (c, e) in enumerate(ATT_PAIRS):
            row = sum_s[4 + 10 * d + q : 5 + 10 * d + q, :]
            att_normal[d, c, e : e + 1, :] = row
            if c != e:
                att_normal[d, e, c : c + 1, :] = row

    def cal_row(t):
        at = 48 + t if t < 24 else 20 + t
        return sum_s[at : at + 1, :]

    for t, (p, q) in enumerate(CAL_PAIRS):
        cal_normal[p, q : q + 1, :] = cal_row(t)
        if p != q:
            cal_normal[q, p : p + 1, :] = cal_row(t)
    for p in range(6):
        cal_rhs[p : p + 1, :] = cal_row(21 + p)


def exchange(blocks, groups):
    return lax.all_to_all(
        blocks, "src", split_axis=0, concat_axis=0, tiled=True, axis_index_groups=groups
    )


def call(kernel, out_shape, scratch, vmem_mib, cost, *args, space=pltpu.VMEM):
    return pl.pallas_call(
        kernel,
        out_shape=out_shape,
        in_specs=[pl.BlockSpec(memory_space=space)] * len(args),
        scratch_shapes=scratch,
        compiler_params=pltpu.CompilerParams(vmem_limit_bytes=vmem_mib * 1024 * 1024),
        cost_estimate=pl.CostEstimate(flops=cost, bytes_accessed=200000, transcendentals=0),
    )(*args)


def shape(*dims):
    return jax.ShapeDtypeStruct(dims, F32)


def local(
    src_partials,
    att_geom,
    spline_frac,
    cal_partials,
    residual,
    weight,
    source_ids,
    knot_ids,
    ccd_ids,
):
    obs = residual.shape[0]
    tm_count = lax.axis_size("tm")
    z_count = lax.axis_size("src")
    rows = (att_geom, spline_frac, cal_partials, residual, weight, knot_ids, ccd_ids)
    send = call(
        pack_kernel,
        shape(tm_count, 2, HIGH // 2 * LANES),
        [
            pltpu.VMEM((HIGH * tm_count, obs), BF16),
            pltpu.VMEM((2 * LANES, obs), BF16),
            pltpu.VMEM((2 * LANES, obs), BF16),
            pltpu.VMEM((HIGH // 2, 2 * tm_count, LANES), F32),
        ]
        + [pltpu.VMEM(x.shape, x.dtype) for x in rows]
        + [pltpu.SemaphoreType.DMA((len(rows),))],
        PACK_MIB,
        1000000000,
        *rows,
        space=pltpu.HBM,
    )
    got = lax.all_to_all(send, "tm", split_axis=0, concat_axis=0, tiled=True)
    src_normal, src_rhs = call(
        source_kernel,
        (shape(5, 5, SRC_DEV), shape(5, SRC_DEV)),
        [pltpu.VMEM((64, obs), BF16)],
        12,
        4000000000,
        src_partials,
        residual,
        weight,
        source_ids,
    )
    got, src_normal, src_rhs = lax.optimization_barrier((got, src_normal, src_rhs))
    chunks = HIGH // 2
    depth = LOW * LANES
    sums = call(
        time_kernel,
        shape(2, 72, SEG),
        [
            pltpu.VMEM((chunks, 2 * tm_count, LANES), F32),
            pltpu.VMEM((chunks, LANES, LANES), F32),
            pltpu.VMEM((chunks, LOW * TERMS_STEP, LANES), F32),
            pltpu.VMEM((chunks, LOW * CAL_STEP, LANES), F32),
            pltpu.VMEM((chunks, 2 * TERMS, depth), BF16),
            pltpu.VMEM((chunks, 64, depth), BF16),
            pltpu.VMEM((chunks, SEG, depth), BF16),
            pltpu.VMEM((chunks, SEG, depth), BF16),
            pltpu.VMEM((48, LANES), F32),
        ],
        24,
        1000000000,
        got,
    )
    pairs = [[2 * g + 1, 2 * g] for g in range(z_count // 2)]
    ranks = [[2 * g + i for g in reversed(range(z_count // 2))] for i in range(2)]
    parts = exchange(sums, pairs)
    parts = call(middle_kernel, shape(z_count // 2, 72, SEG), [], 8, 1000000, parts)
    parts = exchange(parts, ranks)
    att_normal, att_rhs, cal_normal, cal_rhs = call(
        final_kernel,
        (shape(4, 4, 4, SEG), shape(4, SEG), shape(6, 6, SEG), shape(6, SEG)),
        [pltpu.VMEM((72, SEG), F32)],
        8,
        1000000,
        parts,
    )
    return (src_normal, src_rhs, att_normal, att_rhs, cal_normal, cal_rhs)


def solution(mesh):
    both = ("tm", "src")
    in_specs = (
        P(None, both),
        P(None, both),
        P(both),
        P(None, both),
        P(both),
        P(both),
        P(both),
        P(both),
        P(both),
    )
    out_specs = (
        P(None, None, both),
        P(None, both),
        P(None, None, None, "tm"),
        P(None, "tm"),
        P(None, None, "tm"),
        P(None, "tm"),
    )
    return jax.shard_map(local, mesh=mesh, in_specs=in_specs, out_specs=out_specs, check_vma=False)
```
